256 devices in a mesh: row: 16 (over z, core), col: 16 (over x, y).
Axes of the slice: x: 4, y: 4, z: 8, core: 2. Of those that a mesh axis runs over, the one named last changes fastest.
Arguments:
- positions: float32 [3, 98304], P(None, ('row', 'col')), may hold values from -5 to 5
- velocities: float32 [3, 98304], P(None, ('row', 'col')), may hold values from -5 to 5
- accels: float32 [3, 98304], P(None, ('row', 'col')), may hold values from -12 to 12
- jerks: float32 [3, 98304], P(None, ('row', 'col')), may hold values from -6 to 6
- masses: float32 [98304], P(('row', 'col')), may hold values from 0.2 to 5
- star_time: float32 [98304], P(('row', 'col')), may hold values from -0.3 to 0
- block_steps: float32 [1], replicated, may hold values from 0.1 to 0.3
- act_index: int32 [1, 32768], P(None, ('row', 'col')), may hold values from 0 to 383, as said below
- act_count: int32 [1, 256], P(None, ('row', 'col')), may hold values from 1 to 128, 8192 in all within a row
Outputs:
- new_positions: float32 [3, 98304], P(None, ('row', 'col'))
- new_velocities: float32 [3, 98304], P(None, ('row', 'col'))
- new_accels: float32 [3, 98304], P(None, ('row', 'col'))
- new_jerks: float32 [3, 98304], P(None, ('row', 'col'))
The draws below stay inside these ranges and needn't reach their ends.
Inputs may be any that keep to these rules, and one draw needn't show every extreme that they name: `act_index`: in each block step the 128 entries of one device are distinct local star numbers of that device; only the first act_count entries are active. Each row of act_count is one block step; its entries, one for each device, sum to 32 times the number of devices over all devices together.
All inputs are finite; a program needn't handle non-finite values.
Results may differ from the reference program's by a relative error of at most 0.00017.
Values sent between devices are 32-bit elements; how exact they have to be, the bound alone decides.
A program may use at most 64 MiB of HBM per device.

```python
import math
import jax
import jax.numpy as jnp
import numpy as np
from jax import lax

M_DEV = 384
ACT_DEV = 32
CAP = 128
BLOCKS = 1
STARS = 98304
N_ROW = 16
N_COL = 16


def draw_positions(key, part):
    clumps = max(STARS // 32, 8)
    subkeys = jax.random.split(jax.random.fold_in(key, 11), 4)
    member = jax.random.randint(subkeys[0], (STARS,), 0, clumps)
    centres = 0.45 * jax.random.normal(subkeys[1], (3, clumps), jnp.float32)
    heading = jnp.array([0.6, 0.48, 0.64], jnp.float32)
    tail_len = 0.25
    heading = heading / jnp.sqrt(jnp.sum(heading * heading))
    along = jax.random.uniform(subkeys[2], (STARS,), jnp.float32)
    jitter = 0.05 * jax.random.normal(subkeys[3], (3, STARS), jnp.float32)
    spread = centres[:, member] + heading[:, None] * (tail_len * along * along)[None, :] + jitter
    return jnp.clip(spread, -5.0, 5.0).astype(jnp.float32)


def draw_act_index(key, part):
    subkeys = jax.random.split(jax.random.fold_in(key, 7), BLOCKS * N_ROW * N_COL)
    orders = jax.vmap(lambda single: jax.random.permutation(single, M_DEV)[:CAP])(subkeys)
    return orders.reshape(BLOCKS, N_ROW * N_COL * CAP).astype(jnp.int32)


def block_levels(rng, shape, cuts, smallest, top_value):
    gain = 1.0
    for axis_at, parts in cuts:
        steps = jax.random.uniform(jax.random.fold_in(jax.random.fold_in(rng, 6), axis_at), (parts,), jnp.float32, smallest / len(cuts), top_value / len(cuts))
        gain = gain * jnp.repeat(jnp.exp(steps), shape[axis_at] // parts).reshape((-1,) + (1,) * (len(shape) - 1 - axis_at))
    return gain


def length_profile(amount, total, limit, slope):
    loads = [(1 << 20) // math.isqrt(grade ** slope) + 1 for grade in range(2, amount + 1)]
    rest, given = total - limit - (amount - 1), [1] * (amount - 1)
    while rest > 0:
        movable = [i for i in range(amount - 1) if given[i] < limit]
        pool, remaining = sum([loads[i] for i in movable]), rest
        for i in movable:
            more = min(limit - given[i], max(1, remaining * loads[i] // pool), rest)
            given[i] = given[i] + more
            rest = rest - more
    return np.array([limit] + given)


def ragged_sizes(rng, amount, total, most, slope):
    if amount == 2:
        one = jax.random.randint(rng, (), max(1, total - most), min(most, total - 1) + 1)
        return jnp.stack([one, total - one])
    tallies = jnp.asarray(length_profile(amount, total, most, slope), jnp.int32)
    pairs = (amount - 1) // 2
    source_of, taker = tallies[1:1 + 2 * pairs:2], tallies[2:2 + 2 * pairs:2]
    room = jnp.minimum(source_of - 1, most - taker)
    shifted = jax.random.randint(jax.random.fold_in(rng, 1), (pairs,), 0, 1 << 20) % (room + 1)
    tallies = tallies.at[1:1 + 2 * pairs:2].set(source_of - shifted).at[2:2 + 2 * pairs:2].set(taker + shifted)
    return tallies[jax.random.permutation(jax.random.fold_in(rng, 2), amount)]


def noise(own_key, dims, width, reach, shards=(), kind=jnp.bfloat16):
    drawn = jax.random.normal(own_key, dims, jnp.float32) * width
    if len(shards) > 0:
        drawn = block_levels(own_key, dims, shards, -0.22, 0.18) * drawn
    return jnp.clip(drawn, min=-reach, max=reach).astype(kind)


def setup_inputs(seed: int = 0) -> dict:
    splits = jax.random.split(jax.random.key(seed), 10)
    positions = draw_positions(jax.random.fold_in(splits[9], 71), 0)
    velocities = noise(splits[1], (3, STARS), 1.0, 5.0, ((1, 256),), jnp.float32)
    accels = noise(splits[2], (3, STARS), 2.0, 12.0, ((1, 256),), jnp.float32)
    jerks = noise(splits[3], (3, STARS), 1.0, 6.0, ((1, 256),), jnp.float32)
    masses = jnp.clip(jnp.exp(math.log(5.0) - 3.218876 * jax.random.uniform(splits[4], (STARS,), jnp.float32) ** block_levels(splits[4], (STARS,), ((0, 256),), -0.2, 0.2)), 0.2, 5.0)
    star_time = jnp.clip(-0.3 + 0.3 * jax.random.uniform(splits[5], (STARS,), jnp.float32) ** block_levels(splits[5], (STARS,), ((0, 256),), -0.2, 0.2), -0.3, 0.0)
    block_steps = jnp.clip(jax.random.uniform(splits[6], (BLOCKS,), jnp.float32, 0.1, 0.3), 0.1, 0.3)
    act_index = draw_act_index(jax.random.fold_in(splits[9], 71), 0)
    act_count = jax.vmap(lambda own: ragged_sizes(own, N_ROW * N_COL, ACT_DEV * N_ROW * N_COL, CAP, 2))(jax.random.split(splits[8], BLOCKS)).reshape((BLOCKS, N_ROW * N_COL)).astype(jnp.int32)
    return dict(positions=positions, velocities=velocities, accels=accels, jerks=jerks, masses=masses, star_time=star_time, block_steps=block_steps, act_index=act_index, act_count=act_count)


SOFTENING = 0.0025
GRAVITY = 8.0

def predict(positions, velocities, accels, jerks, elapsed):
    square = elapsed * elapsed
    pred_pos = positions + velocities * elapsed + accels * (square * 0.5) + jerks * (square * elapsed / 6.0)
    pred_vel = velocities + accels * elapsed + jerks * (square * 0.5)
    return (pred_pos, pred_vel)

def pair_forces(target_pos, target_vel, source_pos, source_vel, source_mass, strength):
    separation = source_pos[:, None, :] - target_pos[:, :, None]
    relvel = source_vel[:, None, :] - target_vel[:, :, None]
    soft_sq = lax.optimization_barrier(jnp.sum(separation * separation, axis=0)) + SOFTENING
    inverse = lax.rsqrt(soft_sq)
    weight = (source_mass * strength)[None, :] * inverse * inverse * inverse
    radial = lax.optimization_barrier(jnp.sum(separation * relvel, axis=0))
    factor = 3.0 * radial / soft_sq * weight
    accel = lax.optimization_barrier(jnp.sum(weight[None] * separation, axis=2))
    jerk = lax.optimization_barrier(jnp.sum(weight[None] * relvel - factor[None] * separation, axis=2))
    return jnp.concatenate([accel, jerk], axis=0)

def blocked_forces(target_pos, target_vel, source_pos, source_vel, source_mass, strength, block_len):
    total = target_pos.shape[1]
    nblocks = total // block_len
    pos_blocks = target_pos.reshape(3, nblocks, block_len).transpose(1, 0, 2)
    vel_blocks = target_vel.reshape(3, nblocks, block_len).transpose(1, 0, 2)
    result = lax.map(lambda target_pair: pair_forces(target_pair[0], target_pair[1], source_pos, source_vel, source_mass, strength), (pos_blocks, vel_blocks))
    return result.transpose(1, 0, 2).reshape(6, total)

def correct(pred_pos, pred_vel, old_acc, old_jerk, new_acc, new_jerk, span):
    change = old_acc - new_acc
    snap_term = -6.0 * change - span * (4.0 * old_jerk + 2.0 * new_jerk)
    crack_term = 12.0 * change + 6.0 * span * (old_jerk + new_jerk)
    out_pos = pred_pos + span * span * (snap_term / 24.0 + crack_term / 120.0)
    out_vel = pred_vel + span * (snap_term / 6.0 + crack_term / 24.0)
    return (out_pos, out_vel)

def reference(positions, velocities, accels, jerks, masses, star_time, block_steps, act_index, act_count):
    star_count = positions.shape[1]
    devices = act_count.shape[1]
    capacity = act_index.shape[1] // devices
    per_dev = star_count // devices
    strength = GRAVITY / star_count
    total_act = ACT_DEV * devices
    block_len = math.gcd(32, total_act)
    slot_ids = jnp.arange(capacity, dtype=jnp.int32)
    bases = jnp.arange(devices, dtype=jnp.int32) * per_dev
    clock = jnp.float32(0.0)
    for section in range(BLOCKS):
        clock = clock + block_steps[section]
        pred_pos, pred_vel = predict(positions, velocities, accels, jerks, clock - star_time)
        counts = act_count[section]
        active = slot_ids[None, :] < counts[:, None]
        global_ids = act_index[section].reshape(devices, capacity) + bases[:, None]
        offsets = jnp.cumsum(counts) - counts
        slot_rank = offsets[:, None] + slot_ids[None, :]
        target_slot = jnp.where(active, slot_rank, total_act).reshape(-1).astype(jnp.int32)
        chosen = jnp.zeros((total_act,), jnp.int32).at[target_slot].set(global_ids.reshape(-1).astype(jnp.int32), mode='drop')
        target_pos = pred_pos[:, chosen]
        target_vel = pred_vel[:, chosen]
        forces = blocked_forces(target_pos, target_vel, pred_pos, pred_vel, masses, strength, block_len)
        new_acc = forces[:3]
        new_jerk = forces[3:]
        span = clock - star_time[chosen]
        out_pos, out_vel = correct(target_pos, target_vel, accels[:, chosen], jerks[:, chosen], new_acc, new_jerk, span)
        positions = positions.at[:, chosen].set(out_pos)
        velocities = velocities.at[:, chosen].set(out_vel)
        accels = accels.at[:, chosen].set(new_acc)
        jerks = jerks.at[:, chosen].set(new_jerk)
        star_time = star_time.at[chosen].set(clock)
    return (positions, velocities, accels, jerks)
```

```python
import functools

import jax
import jax.numpy as jnp
from jax import lax
from jax.experimental import pallas as pl
from jax.experimental.pallas import tpu as pltpu
from jax.sharding import PartitionSpec as P

SOFTENING = 0.0025
GRAVITY = 8.0
LANES = 128
ROWS = 2
MESH = pl.DeviceIdType.MESH
HIGHEST = lax.Precision.HIGHEST


def predict(pos, vel, acc, jerk, elapsed):
    square = elapsed * elapsed
    pred_pos = pos + vel * elapsed + acc * (square * 0.5) + jerk * (square * elapsed / 6.0)
    pred_vel = vel + acc * elapsed + jerk * (square * 0.5)
    return pred_pos, pred_vel


def peer_a(k, n_col):
    group = ROWS * n_col
    row, col = lax.axis_index("row"), lax.axis_index("col")
    mine = (row % ROWS) * n_col + col
    other = (mine + k) % group
    return (row // ROWS) * ROWS + other // n_col, other % n_col


def peer_b(k, n_row):
    group = n_row // ROWS
    row, col = lax.axis_index("row"), lax.axis_index("col")
    return ((row // ROWS + k) % group) * ROWS + row % ROWS, col


def one_hot(index_row, count, stars):
    star = lax.broadcasted_iota(jnp.int32, (stars, LANES), 0)
    slot = lax.broadcasted_iota(jnp.int32, (stars, LANES), 1)
    return jnp.where((star == index_row) & (slot < count), 1.0, 0.0)


def exchange_kernel(
    n_row, n_col, strength,
    step_ref, count_ref, pos_ref, vel_ref, acc_ref, jerk_ref, mass_ref, time_ref, index_ref,
    tgt_ref, src_ref, cnt_ref,
    send_a, recv_a, send_b, recv_b,
):
    n_a, n_b = ROWS * n_col, n_row // ROWS
    barrier = pltpu.get_barrier_semaphore()

    def greet_a(k, _):
        pl.semaphore_signal(barrier, inc=1, device_id=peer_a(k, n_col), device_id_type=MESH)
        return 0

    def greet_b(k, _):
        pl.semaphore_signal(barrier, inc=1, device_id=peer_b(k, n_row), device_id_type=MESH)
        return 0

    lax.fori_loop(1, n_a, greet_a, 0)
    lax.fori_loop(1, n_b, greet_b, 0)

    stars = pos_ref.shape[1]
    elapsed = step_ref[0] - time_ref[...].reshape(1, stars)
    pred_pos, pred_vel = predict(pos_ref[...], vel_ref[...], acc_ref[...], jerk_ref[...], elapsed)
    weight = mass_ref[...].reshape(1, stars) * strength
    packet = jnp.concatenate([pred_pos, pred_vel, weight, jnp.zeros_like(weight)], axis=0)
    src_ref[0] = packet
    count = count_ref[0, 0]
    chosen = jnp.dot(
        packet, one_hot(index_ref[...], LANES, stars), precision=HIGHEST,
        preferred_element_type=jnp.float32,
    )
    comp = lax.broadcasted_iota(jnp.int32, (8, LANES), 0)
    tgt_ref[0] = jnp.where(comp == 6, count.astype(jnp.float32), chosen)

    pl.semaphore_wait(barrier, n_a + n_b - 2)

    def copy_b(k):
        return pltpu.make_async_remote_copy(
            src_ref=src_ref.at[0], dst_ref=src_ref.at[n_b - k],
            send_sem=send_b.at[k], recv_sem=recv_b.at[n_b - k],
            device_id=peer_b(k, n_row), device_id_type=MESH,
        )

    def copy_a(k):
        return pltpu.make_async_remote_copy(
            src_ref=tgt_ref.at[0], dst_ref=tgt_ref.at[n_a - k],
            send_sem=send_a.at[k], recv_sem=recv_a.at[n_a - k],
            device_id=peer_a(k, n_col), device_id_type=MESH,
        )

    def start_b(k, _):
        copy_b(k).start()
        return 0

    def start_a(k, _):
        copy_a(k).start()
        return 0

    def wait_b(k, _):
        copy_b(k).wait()
        return 0

    def wait_a(k, _):
        copy_a(k).wait()
        return 0

    lax.fori_loop(1, n_b, start_b, 0)
    lax.fori_loop(1, n_a, start_a, 0)
    lax.fori_loop(1, n_a, wait_a, 0)
    lane = lax.broadcasted_iota(jnp.int32, (1, LANES), 1)
    counts = jnp.zeros((1, LANES), jnp.float32)
    for k in range(n_a):
        counts = jnp.where(lane == k, tgt_ref[k, 6:7, :], counts)
    cnt_ref[...] = counts.astype(jnp.int32)
    lax.fori_loop(1, n_b, wait_b, 0)


def force_kernel(cnt_ref, tgt_ref, src_ref, out_ref, dense, dense_t, res_t, srcb, offs):
    n_a, n_b, stars = tgt_ref.shape[0], src_ref.shape[0], src_ref.shape[2]
    per = stars // LANES
    chunks = n_b * per

    for b in range(n_b):
        for p in range(per):
            for c in range(7):
                row = src_ref[b, c : c + 1, p * LANES : (p + 1) * LANES]
                srcb[c, b * per + p] = jnp.broadcast_to(row, (8, LANES))

    lane = lax.broadcasted_iota(jnp.int32, (8, LANES), 1)

    def compact(k, off):
        tile, shift = off // LANES, off % LANES
        rolled = pltpu.roll(tgt_ref[k], shift, 1)
        dense[tile] = jnp.where(lane >= shift, rolled, dense[tile])
        dense[tile + 1] = rolled
        offs[k] = off
        return off + cnt_ref[0, k]

    total = lax.fori_loop(0, n_a, compact, jnp.int32(0))
    tiles = (total + LANES - 1) // LANES

    def turn(t, _):
        dense_t[pl.ds(pl.multiple_of(t * LANES, LANES), LANES), 0:8] = dense[t].T
        return 0

    lax.fori_loop(0, tiles, turn, 0)
    blocks = (total + 15) // 16

    def block(i, _):
        base = pl.multiple_of(i * 16, 16)
        own = []
        for h in range(2):
            rows = dense_t[pl.ds(base + 8 * h, 8), :]
            own.append([jnp.broadcast_to(rows[:, c : c + 1], (8, LANES)) for c in range(6)])
        sums = [[jnp.zeros((8, LANES), jnp.float32) for _ in range(6)] for _ in range(2)]
        for j in range(chunks):
            s = [srcb[c, j] for c in range(7)]
            for h in range(2):
                d = [s[c] - own[h][c] for c in range(6)]
                q = d[0] * d[0] + d[1] * d[1] + d[2] * d[2] + SOFTENING
                inv = lax.rsqrt(q)
                inv2 = inv * inv
                w = s[6] * inv * inv2
                radial = d[0] * d[3] + d[1] * d[4] + d[2] * d[5]
                f = (3.0 * radial) * inv2
                for c in range(3):
                    wr = w * d[c]
                    sums[h][c] = sums[h][c] + wr
                    sums[h][3 + c] = sums[h][3 + c] + (w * d[3 + c] - f * wr)
        for h in range(2):
            res = jnp.zeros((8, LANES), jnp.float32)
            for c in range(6):
                res = jnp.where(lane == c, jnp.sum(sums[h][c], axis=1, keepdims=True), res)
            res_t[pl.ds(base + 8 * h, 8), :] = res
        return 0

    lax.fori_loop(0, blocks, block, 0)

    def back(t, _):
        dense[t] = res_t[pl.ds(pl.multiple_of(t * LANES, LANES), LANES), :].T[0:8]
        return 0

    lax.fori_loop(0, tiles, back, 0)

    def spread(k, _):
        off = offs[k]
        tile, shift = off // LANES, off % LANES
        both = jnp.where(lane >= shift, dense[tile], dense[tile + 1])
        out_ref[k] = pltpu.roll(both, (LANES - shift) % LANES, 1)
        return 0

    lax.fori_loop(0, n_a, spread, 0)


def return_kernel(
    n_row, n_col,
    step_ref, count_ref, part_ref, pos_ref, vel_ref, acc_ref, jerk_ref, time_ref, index_ref,
    new_pos, new_vel, new_acc, new_jerk,
    inbox, send_sem, recv_sem,
):
    n_a = ROWS * n_col
    barrier = pltpu.get_barrier_semaphore()

    def greet(k, _):
        pl.semaphore_signal(barrier, inc=1, device_id=peer_a(k, n_col), device_id_type=MESH)
        return 0

    lax.fori_loop(1, n_a, greet, 0)
    stars = pos_ref.shape[1]
    clock = step_ref[0]
    span = clock - time_ref[...].reshape(1, stars)
    pos, vel, acc, jerk = pos_ref[...], vel_ref[...], acc_ref[...], jerk_ref[...]
    pred_pos, pred_vel = predict(pos, vel, acc, jerk, span)
    pick = one_hot(index_ref[...], count_ref[0, 0], stars)
    pl.semaphore_wait(barrier, n_a - 1)

    def copy(k):
        return pltpu.make_async_remote_copy(
            src_ref=part_ref.at[k], dst_ref=inbox.at[n_a - k],
            send_sem=send_sem.at[k], recv_sem=recv_sem.at[n_a - k],
            device_id=peer_a(k, n_col), device_id_type=MESH,
        )

    def start(k, _):
        copy(k).start()
        return 0

    def wait(k, _):
        copy(k).wait()
        return 0

    lax.fori_loop(1, n_a, start, 0)
    lax.fori_loop(1, n_a, wait, 0)
    total = part_ref[0]
    for k in range(1, n_a):
        total = total + inbox[k]
    comp = lax.broadcasted_iota(jnp.int32, (8, LANES), 0)
    total = jnp.where(comp < 6, total, 1.0)
    placed = lax.dot_general(
        total, pick, (((1,), (1,)), ((), ())), precision=HIGHEST,
        preferred_element_type=jnp.float32,
    )
    active = placed[6:7] > 0.5
    acc1, jerk1 = placed[0:3], placed[3:6]
    change = acc - acc1
    snap = -6.0 * change - span * (4.0 * jerk + 2.0 * jerk1)
    crack = 12.0 * change + 6.0 * span * (jerk + jerk1)
    out_pos = pred_pos + span * span * (snap / 24.0 + crack / 120.0)
    out_vel = pred_vel + span * (snap / 6.0 + crack / 24.0)
    new_pos[...] = jnp.where(active, out_pos, pos)
    new_vel[...] = jnp.where(active, out_vel, vel)
    new_acc[...] = jnp.where(active, acc1, acc)
    new_jerk[...] = jnp.where(active, jerk1, jerk)


def solution(mesh):
    n_row, n_col = mesh.shape["row"], mesh.shape["col"]
    n_a, n_b = ROWS * n_col, n_row // ROWS
    vmem = pl.BlockSpec(memory_space=pltpu.VMEM)
    smem = pl.BlockSpec(memory_space=pltpu.SMEM)
    f32 = jnp.float32

    def per_device(pos, vel, acc, jerk, mass, time, steps, index, count):
        stars = pos.shape[1]
        strength = GRAVITY / (stars * n_row * n_col)
        tgt, src, cnt = pl.pallas_call(
            functools.partial(exchange_kernel, n_row, n_col, strength),
            out_shape=(
                jax.ShapeDtypeStruct((n_a, 8, LANES), f32),
                jax.ShapeDtypeStruct((n_b, 8, stars), f32),
                jax.ShapeDtypeStruct((1, LANES), jnp.int32),
            ),
            in_specs=[smem, smem] + [vmem] * 7,
            out_specs=(vmem, vmem, vmem),
            scratch_shapes=[
                pltpu.SemaphoreType.DMA((n_a,)),
                pltpu.SemaphoreType.DMA((n_a,)),
                pltpu.SemaphoreType.DMA((n_b,)),
                pltpu.SemaphoreType.DMA((n_b,)),
            ],
            compiler_params=pltpu.CompilerParams(collective_id=0, has_side_effects=True),
            name="exchange",
        )(steps, count, pos, vel, acc, jerk, mass, time, index)
        chunks = n_b * stars // LANES
        part = pl.pallas_call(
            force_kernel,
            out_shape=jax.ShapeDtypeStruct((n_a, 8, LANES), f32),
            in_specs=[smem, vmem, vmem],
            out_specs=vmem,
            scratch_shapes=[
                pltpu.VMEM((n_a + 2, 8, LANES), f32),
                pltpu.VMEM(((n_a + 2) * LANES, LANES), f32),
                pltpu.VMEM(((n_a + 2) * LANES, LANES), f32),
                pltpu.VMEM((7, chunks, 8, LANES), f32),
                pltpu.SMEM((n_a,), jnp.int32),
            ],
            name="forces",
        )(cnt, tgt, src)
        return pl.pallas_call(
            functools.partial(return_kernel, n_row, n_col),
            out_shape=(jax.ShapeDtypeStruct(pos.shape, f32),) * 4,
            in_specs=[smem, smem] + [vmem] * 7,
            out_specs=(vmem,) * 4,
            scratch_shapes=[
                pltpu.VMEM((n_a, 8, LANES), f32),
                pltpu.SemaphoreType.DMA((n_a,)),
                pltpu.SemaphoreType.DMA((n_a,)),
            ],
            compiler_params=pltpu.CompilerParams(collective_id=1, has_side_effects=True),
            name="returns",
        )(steps, count, part, pos, vel, acc, jerk, time, index)

    both = ("row", "col")
    state = P(None, both)
    return jax.shard_map(
        per_device,
        mesh=mesh,
        in_specs=(state, state, state, state, P(both), P(both), P(), state, state),
        out_specs=(state, state, state, state),
        check_vma=False,
    )
```

```python
import functools

import jax
import jax.numpy as jnp
from jax import lax
from jax.experimental import pallas as pl
from jax.experimental.pallas import tpu as pltpu
from jax.sharding import PartitionSpec as P

SOFTENING = 0.0025
GRAVITY = 8.0
LANES = 128
ROWS = 2
AHEAD = 2
MESH = pl.DeviceIdType.MESH
HIGHEST = lax.Precision.HIGHEST


def predict(pos, vel, acc, jerk, elapsed):
    square = elapsed * elapsed
    pred_pos = pos + vel * elapsed + acc * (square * 0.5) + jerk * (square * elapsed / 6.0)
    pred_vel = vel + acc * elapsed + jerk * (square * 0.5)
    return pred_pos, pred_vel


def peer_a(k, n_col):
    group = ROWS * n_col
    row, col = lax.axis_index("row"), lax.axis_index("col")
    mine = (row % ROWS) * n_col + col
    other = (mine + k) % group
    return (row // ROWS) * ROWS + other // n_col, other % n_col


def peer_b(k, n_row):
    group = n_row // ROWS
    row, col = lax.axis_index("row"), lax.axis_index("col")
    return ((row // ROWS + k) % group) * ROWS + row % ROWS, col


def one_hot(index_row, count, stars):
    star = lax.broadcasted_iota(jnp.int32, (stars, LANES), 0)
    slot = lax.broadcasted_iota(jnp.int32, (stars, LANES), 1)
    return jnp.where((star == index_row) & (slot < count), 1.0, 0.0)


def exchange_kernel(
    n_row, n_col, strength,
    step_ref, count_ref, pos_ref, vel_ref, acc_ref, jerk_ref, mass_ref, time_ref, index_ref,
    tgt_ref, src_ref, cnt_ref,
    send_a, recv_a, send_b, recv_b,
):
    n_a, n_b = ROWS * n_col, n_row // ROWS
    barrier = pltpu.get_barrier_semaphore()

    def greet_a(k, _):
        pl.semaphore_signal(barrier, inc=1, device_id=peer_a(k, n_col), device_id_type=MESH)
        return 0

    def greet_b(k, _):
        pl.semaphore_signal(barrier, inc=1, device_id=peer_b(k, n_row), device_id_type=MESH)
        return 0

    lax.fori_loop(1, n_a, greet_a, 0)
    lax.fori_loop(1, n_b, greet_b, 0)

    stars = pos_ref.shape[1]
    elapsed = step_ref[0] - time_ref[...].reshape(1, stars)
    pred_pos, pred_vel = predict(pos_ref[...], vel_ref[...], acc_ref[...], jerk_ref[...], elapsed)
    weight = mass_ref[...].reshape(1, stars) * strength
    packet = jnp.concatenate([pred_pos, pred_vel, weight, jnp.zeros_like(weight)], axis=0)
    src_ref[0] = packet
    count = count_ref[0, 0]
    chosen = jnp.dot(
        packet, one_hot(index_ref[...], LANES, stars), precision=HIGHEST,
        preferred_element_type=jnp.float32,
    )
    comp = lax.broadcasted_iota(jnp.int32, (8, LANES), 0)
    tgt_ref[0] = jnp.where(comp == 6, count.astype(jnp.float32), chosen)

    pl.semaphore_wait(barrier, n_a + n_b - 2)

    def copy_b(k):
        return pltpu.make_async_remote_copy(
            src_ref=src_ref.at[0], dst_ref=src_ref.at[n_b - k],
            send_sem=send_b.at[k], recv_sem=recv_b.at[n_b - k],
            device_id=peer_b(k, n_row), device_id_type=MESH,
        )

    def copy_a(k):
        return pltpu.make_async_remote_copy(
            src_ref=tgt_ref.at[0], dst_ref=tgt_ref.at[n_a - k],
            send_sem=send_a.at[k], recv_sem=recv_a.at[n_a - k],
            device_id=peer_a(k, n_col), device_id_type=MESH,
        )

    def start_b(k, _):
        copy_b(k).start()
        return 0

    def start_a(k, _):
        copy_a(k).start()
        return 0

    def wait_b(k, _):
        copy_b(k).wait()
        return 0

    def wait_a(k, _):
        copy_a(k).wait()
        return 0

    lax.fori_loop(1, n_b, start_b, 0)
    lax.fori_loop(1, n_a, start_a, 0)
    lax.fori_loop(1, n_a, wait_a, 0)
    lane = lax.broadcasted_iota(jnp.int32, (1, LANES), 1)
    counts = jnp.zeros((1, LANES), jnp.float32)
    for k in range(n_a):
        counts = jnp.where(lane == k, tgt_ref[k, 6:7, :], counts)
    cnt_ref[...] = counts.astype(jnp.int32)
    lax.fori_loop(1, n_b, wait_b, 0)


def split3(x):
    high = x.astype(jnp.bfloat16).astype(jnp.float32)
    rest = x - high
    mid = rest.astype(jnp.bfloat16).astype(jnp.float32)
    return high, mid, rest - mid


def force_kernel(
    cnt_ref, tgt_ref, src_ref, out_ref, dense, src_t, spot, packed, offs
):
    n_a, n_b, stars = tgt_ref.shape[0], src_ref.shape[0], src_ref.shape[2]
    per = stars // LANES
    parts = n_b * per
    f32, bf16 = jnp.float32, jnp.bfloat16
    comp = lax.broadcasted_iota(jnp.int32, (8, LANES), 0)
    lane = lax.broadcasted_iota(jnp.int32, (8, LANES), 1)
    one = jnp.ones((1, LANES), f32)

    def piece(j):
        b, p = j // per, j % per
        return src_ref[b, :, p * LANES : (p + 1) * LANES]

    total = piece(0)
    for j in range(1, parts):
        total = total + piece(j)
    middle = jnp.sum(total, axis=1, keepdims=True) * (1.0 / (parts * LANES))
    middle = jnp.where(comp < 6, jnp.broadcast_to(middle, (8, LANES)), 0.0)

    for j in range(parts):
        state = piece(j) - middle
        dot_xv = state[0:1] * state[3:4] + state[1:2] * state[4:5] + state[2:3] * state[5:6]
        high, mid, low = split3(jnp.concatenate([state[3:6], state[0:3], dot_xv, one], axis=0))
        rows = jnp.concatenate(
            [high, mid, high, mid, low, high, state, jnp.zeros((8, LANES), f32)], axis=0
        )
        cols = rows.T
        src_t[j * LANES : (j + 1) * LANES, :] = cols.astype(bf16)
        for g in range(LANES // 8):
            for c in range(3):
                spot[j * (LANES // 8) + g, c] = jnp.broadcast_to(
                    cols[8 * g : 8 * g + 8, 48 + c : 49 + c], (8, LANES)
                )
        mass = state[6:7]
        moment = jnp.where(comp < 6, state * mass, jnp.where(comp == 6, state, 0.0))
        high, mid, low = split3(moment)
        rows = jnp.concatenate([high, mid, low, jnp.zeros((8, LANES), f32)], axis=0).astype(bf16)
        packed[j, :, 0:LANES] = rows
        packed[j, :, LANES : 2 * LANES] = rows

    def compact(k, off):
        tile, shift = off // LANES, off % LANES
        rolled = pltpu.roll(tgt_ref[k], shift, 1)
        dense[tile] = jnp.where(lane >= shift, rolled, dense[tile])
        dense[tile + 1] = rolled
        offs[k] = off
        return off + cnt_ref[0, k]

    count = lax.fori_loop(0, n_a, compact, jnp.int32(0))
    tiles = (count + LANES - 1) // LANES

    def tile_step(t, _):
        state = dense[t] - middle
        dot_xv = state[0:1] * state[3:4] + state[1:2] * state[4:5] + state[2:3] * state[5:6]
        high, mid, low = split3(jnp.concatenate([-state[0:6], one, dot_xv], axis=0))
        pair = jnp.concatenate(
            [high, high, mid, mid, high, low, jnp.zeros((16, LANES), f32)], axis=0
        ).astype(bf16)
        own = [jnp.broadcast_to(state[c : c + 1], (8, LANES)) for c in range(3)]

        def radial_of(c):
            return jnp.dot(
                src_t[c * LANES : (c + 1) * LANES, :], pair, preferred_element_type=f32
            )

        def weights_of(c, radial):
            tiles_of = [[], [], [], []]
            for g in range(8):
                pulls, twists = [], []
                for h in range(2):
                    at = c * 16 + 2 * g + h
                    dx = spot[at, 0] - own[0]
                    dy = spot[at, 1] - own[1]
                    dz = spot[at, 2] - own[2]
                    q = dx * dx + (dy * dy + (dz * dz + SOFTENING))
                    inv = lax.rsqrt(q)
                    inv2 = inv * inv
                    pull = inv * inv2
                    pulls.append(pull)
                    twists.append((radial[16 * g + 8 * h : 16 * g + 8 * h + 8] * inv2) * pull)
                for s, both in enumerate((pulls, twists)):
                    full = jnp.concatenate(both, axis=0)
                    high = full.astype(bf16)
                    tiles_of[s].append(high)
                    tiles_of[2 + s].append((full - high.astype(f32)).astype(bf16))
            cols = [jnp.concatenate(x, axis=0) for x in tiles_of]
            return jnp.concatenate(
                [jnp.concatenate(cols[0:2], axis=1), jnp.concatenate(cols[2:4], axis=1)], axis=0
            )

        acc = jnp.zeros((32, 2 * LANES), f32)
        ahead = [radial_of(c) for c in range(AHEAD)]
        right = None
        for c in range(parts):
            if c + AHEAD < parts:
                ahead.append(radial_of(c + AHEAD))
            last, right = right, weights_of(c, ahead[c])
            if last is not None:
                acc = acc + jnp.dot(packed[c - 1], last, preferred_element_type=f32)
        acc = acc + jnp.dot(packed[parts - 1], right, preferred_element_type=f32)
        acc = acc[0:8] + (acc[8:16] + acc[16:24])
        pull, twist = acc[:, :LANES], acc[:, LANES:]
        force = pull - state * pull[6:7]
        tide = twist - state * twist[6:7]
        jerk = force[3:6] - 3.0 * tide[0:3]
        dense[t] = jnp.concatenate([force[0:3], jerk, jnp.zeros((2, LANES), f32)], axis=0)
        return 0

    lax.fori_loop(0, tiles, tile_step, 0)

    def spread(k, _):
        off = offs[k]
        tile, shift = off // LANES, off % LANES
        both = jnp.where(lane >= shift, dense[tile], dense[tile + 1])
        out_ref[k] = pltpu.roll(both, (LANES - shift) % LANES, 1)
        return 0

    lax.fori_loop(0, n_a, spread, 0)


def return_kernel(
    n_row, n_col,
    step_ref, count_ref, part_ref, pos_ref, vel_ref, acc_ref, jerk_ref, time_ref, index_ref,
    new_pos, new_vel, new_acc, new_jerk,
    inbox, send_sem, recv_sem,
):
    n_a = ROWS * n_col
    barrier = pltpu.get_barrier_semaphore()

    def greet(k, _):
        pl.semaphore_signal(barrier, inc=1, device_id=peer_a(k, n_col), device_id_type=MESH)
        return 0

    lax.fori_loop(1, n_a, greet, 0)
    stars = pos_ref.shape[1]
    clock = step_ref[0]
    span = clock - time_ref[...].reshape(1, stars)
    pos, vel, acc, jerk = pos_ref[...], vel_ref[...], acc_ref[...], jerk_ref[...]
    pred_pos, pred_vel = predict(pos, vel, acc, jerk, span)
    pick = one_hot(index_ref[...], count_ref[0, 0], stars)
    pl.semaphore_wait(barrier, n_a - 1)

    def copy(k):
        return pltpu.make_async_remote_copy(
            src_ref=part_ref.at[k], dst_ref=inbox.at[n_a - k],
            send_sem=send_sem.at[k], recv_sem=recv_sem.at[n_a - k],
            device_id=peer_a(k, n_col), device_id_type=MESH,
        )

    def start(k, _):
        copy(k).start()
        return 0

    def wait(k, _):
        copy(k).wait()
        return 0

    lax.fori_loop(1, n_a, start, 0)
    lax.fori_loop(1, n_a, wait, 0)
    total = part_ref[0]
    for k in range(1, n_a):
        total = total + inbox[k]
    comp = lax.broadcasted_iota(jnp.int32, (8, LANES), 0)
    total = jnp.where(comp < 6, total, 1.0)
    placed = lax.dot_general(
        total, pick, (((1,), (1,)), ((), ())), precision=HIGHEST,
        preferred_element_type=jnp.float32,
    )
    active = placed[6:7] > 0.5
    acc1, jerk1 = placed[0:3], placed[3:6]
    change = acc - acc1
    snap = -6.0 * change - span * (4.0 * jerk + 2.0 * jerk1)
    crack = 12.0 * change + 6.0 * span * (jerk + jerk1)
    out_pos = pred_pos + span * span * (snap / 24.0 + crack / 120.0)
    out_vel = pred_vel + span * (snap / 6.0 + crack / 24.0)
    new_pos[...] = jnp.where(active, out_pos, pos)
    new_vel[...] = jnp.where(active, out_vel, vel)
    new_acc[...] = jnp.where(active, acc1, acc)
    new_jerk[...] = jnp.where(active, jerk1, jerk)


def solution(mesh):
    n_row, n_col = mesh.shape["row"], mesh.shape["col"]
    n_a, n_b = ROWS * n_col, n_row // ROWS
    vmem = pl.BlockSpec(memory_space=pltpu.VMEM)
    smem = pl.BlockSpec(memory_space=pltpu.SMEM)
    f32 = jnp.float32

    def per_device(pos, vel, acc, jerk, mass, time, steps, index, count):
        stars = pos.shape[1]
        strength = GRAVITY / (stars * n_row * n_col)
        tgt, src, cnt = pl.pallas_call(
            functools.partial(exchange_kernel, n_row, n_col, strength),
            out_shape=(
                jax.ShapeDtypeStruct((n_a, 8, LANES), f32),
                jax.ShapeDtypeStruct((n_b, 8, stars), f32),
                jax.ShapeDtypeStruct((1, LANES), jnp.int32),
            ),
            in_specs=[smem, smem] + [vmem] * 7,
            out_specs=(vmem, vmem, vmem),
            scratch_shapes=[
                pltpu.SemaphoreType.DMA((n_a,)),
                pltpu.SemaphoreType.DMA((n_a,)),
                pltpu.SemaphoreType.DMA((n_b,)),
                pltpu.SemaphoreType.DMA((n_b,)),
            ],
            compiler_params=pltpu.CompilerParams(collective_id=0, has_side_effects=True),
            name="exchange",
        )(steps, count, pos, vel, acc, jerk, mass, time, index)
        chunks = n_b * stars // LANES
        part = pl.pallas_call(
            force_kernel,
            out_shape=jax.ShapeDtypeStruct((n_a, 8, LANES), f32),
            in_specs=[smem, vmem, vmem],
            out_specs=vmem,
            scratch_shapes=[
                pltpu.VMEM((n_a + 2, 8, LANES), f32),
                pltpu.VMEM((chunks * LANES, 64), jnp.bfloat16),
                pltpu.VMEM((chunks * LANES // 8, 3, 8, LANES), f32),
                pltpu.VMEM((chunks, 32, 2 * LANES), jnp.bfloat16),
                pltpu.SMEM((n_a,), jnp.int32),
            ],
            name="forces",
        )(cnt, tgt, src)
        return pl.pallas_call(
            functools.partial(return_kernel, n_row, n_col),
            out_shape=(jax.ShapeDtypeStruct(pos.shape, f32),) * 4,
            in_specs=[smem, smem] + [vmem] * 7,
            out_specs=(vmem,) * 4,
            scratch_shapes=[
                pltpu.VMEM((n_a, 8, LANES), f32),
                pltpu.SemaphoreType.DMA((n_a,)),
                pltpu.SemaphoreType.DMA((n_a,)),
            ],
            compiler_params=pltpu.CompilerParams(collective_id=1, has_side_effects=True),
            name="returns",
        )(steps, count, part, pos, vel, acc, jerk, time, index)

    both = ("row", "col")
    state = P(None, both)
    return jax.shard_map(
        per_device,
        mesh=mesh,
        in_specs=(state, state, state, state, P(both), P(both), P(), state, state),
        out_specs=(state, state, state, state),
        check_vma=False,
    )
```

```python
import functools

import jax
import jax.numpy as jnp
from jax import lax
from jax.experimental import pallas as pl
from jax.experimental.pallas import tpu as pltpu
from jax.sharding import PartitionSpec as P

SOFTENING = 0.0025
GRAVITY = 8.0
LANES = 128
ROWS = 2
AHEAD = 2
SPAN = 2
MESH = pl.DeviceIdType.MESH
HIGHEST = lax.Precision.HIGHEST


def predict(pos, vel, acc, jerk, elapsed):
    square = elapsed * elapsed
    pred_pos = pos + vel * elapsed + acc * (square * 0.5) + jerk * (square * elapsed / 6.0)
    pred_vel = vel + acc * elapsed + jerk * (square * 0.5)
    return pred_pos, pred_vel


def peer_a(k, n_col):
    group = ROWS * n_col
    row, col = lax.axis_index("row"), lax.axis_index("col")
    mine = (row % ROWS) * n_col + col
    other = (mine + k) % group
    return (row // ROWS) * ROWS + other // n_col, other % n_col


def peer_b(k, n_row):
    group = n_row // ROWS
    row, col = lax.axis_index("row"), lax.axis_index("col")
    return ((row // ROWS + k) % group) * ROWS + row % ROWS, col


def one_hot(index_row, count, stars):
    star = lax.broadcasted_iota(jnp.int32, (stars, LANES), 0)
    slot = lax.broadcasted_iota(jnp.int32, (stars, LANES), 1)
    return jnp.where((star == index_row) & (slot < count), 1.0, 0.0)


def exchange_kernel(
    n_row, n_col, strength,
    step_ref, count_ref, pos_ref, vel_ref, acc_ref, jerk_ref, mass_ref, time_ref, index_ref,
    tgt_ref, src_ref, cnt_ref,
    send_a, recv_a, send_b, recv_b,
):
    n_a, n_b = ROWS * n_col, n_row // ROWS
    barrier = pltpu.get_barrier_semaphore()

    def greet_a(k, _):
        pl.semaphore_signal(barrier, inc=1, device_id=peer_a(k, n_col), device_id_type=MESH)
        return 0

    def greet_b(k, _):
        pl.semaphore_signal(barrier, inc=1, device_id=peer_b(k, n_row), device_id_type=MESH)
        return 0

    lax.fori_loop(1, n_a, greet_a, 0)
    lax.fori_loop(1, n_b, greet_b, 0)

    stars = pos_ref.shape[1]
    elapsed = step_ref[0] - time_ref[...].reshape(1, stars)
    pred_pos, pred_vel = predict(pos_ref[...], vel_ref[...], acc_ref[...], jerk_ref[...], elapsed)
    weight = mass_ref[...].reshape(1, stars) * strength
    packet = jnp.concatenate([pred_pos, pred_vel, weight, jnp.zeros_like(weight)], axis=0)
    src_ref[0] = packet
    count = count_ref[0, 0]
    chosen = jnp.dot(
        packet, one_hot(index_ref[...], LANES, stars), precision=HIGHEST,
        preferred_element_type=jnp.float32,
    )
    comp = lax.broadcasted_iota(jnp.int32, (8, LANES), 0)
    tgt_ref[0] = jnp.where(comp == 6, count.astype(jnp.float32), chosen)

    pl.semaphore_wait(barrier, n_a + n_b - 2)

    def copy_b(k):
        return pltpu.make_async_remote_copy(
            src_ref=src_ref.at[0], dst_ref=src_ref.at[n_b - k],
            send_sem=send_b.at[k], recv_sem=recv_b.at[n_b - k],
            device_id=peer_b(k, n_row), device_id_type=MESH,
        )

    def copy_a(k):
        return pltpu.make_async_remote_copy(
            src_ref=tgt_ref.at[0], dst_ref=tgt_ref.at[n_a - k],
            send_sem=send_a.at[k], recv_sem=recv_a.at[n_a - k],
            device_id=peer_a(k, n_col), device_id_type=MESH,
        )

    def start_b(k, _):
        copy_b(k).start()
        return 0

    def start_a(k, _):
        copy_a(k).start()
        return 0

    def wait_b(k, _):
        copy_b(k).wait()
        return 0

    def wait_a(k, _):
        copy_a(k).wait()
        return 0

    lax.fori_loop(1, n_b, start_b, 0)
    lax.fori_loop(1, n_a, start_a, 0)
    lax.fori_loop(1, n_a, wait_a, 0)
    lane = lax.broadcasted_iota(jnp.int32, (1, LANES), 1)
    counts = jnp.zeros((1, LANES), jnp.float32)
    for k in range(n_a):
        counts = jnp.where(lane == k, tgt_ref[k, 6:7, :], counts)
    cnt_ref[...] = counts.astype(jnp.int32)
    lax.fori_loop(1, n_b, wait_b, 0)


def split3(x):
    high = x.astype(jnp.bfloat16).astype(jnp.float32)
    rest = x - high
    mid = rest.astype(jnp.bfloat16).astype(jnp.float32)
    return high, mid, (rest - mid).astype(jnp.bfloat16).astype(jnp.float32)


def grid3(x):
    coarse = jnp.floor(x * 8.0 + 0.5) * 0.125
    rest = x - coarse
    fine = jnp.floor(rest * 4096.0 + 0.5) * (1.0 / 4096.0)
    return coarse, fine, (rest - fine).astype(jnp.bfloat16).astype(jnp.float32)


def sum3(x):
    return x[0:1] + x[1:2] + x[2:3]


def levels(state):
    xg, xm, xr = grid3(state[0:3])
    vh, vm, vl = split3(state[3:6])
    x, v = xg + xm + xr, vh + vm + vl
    scalars = [
        sum3(x * v),
        sum3(xg * xg + 2.0 * (xg * xm)),
        sum3(xm * xm + 2.0 * (xg * xr) + 2.0 * (xm * xr) + xr * xr),
    ]
    return (xg, xm, xr), (vh, vm, vl), scalars


def source_features(state):
    xs, vs, (s, ab, c) = levels(state)
    one = jnp.ones_like(state[0:1])
    none = jnp.zeros_like(one)
    s, ab, c = split3(s), split3(ab), split3(c)
    g = jnp.concatenate([xs[0], vs[0], s[0], one], axis=0)
    m = jnp.concatenate([xs[1], vs[1], s[1], none], axis=0)
    r = jnp.concatenate([xs[2], vs[2], s[2], none], axis=0)
    e = jnp.concatenate([*ab, one, none, none, none, none], axis=0)
    f = jnp.concatenate([*c, one, one, none, none, none], axis=0)
    return jnp.concatenate([g, g, m, e, g, m, m, r, r, r, f, jnp.zeros_like(f)], axis=0)


def target_features(state):
    xs, vs, (s, ab, c) = levels(state)
    one = jnp.ones_like(state[0:1])
    none = jnp.zeros_like(one)
    void = jnp.zeros_like(state[0:3])
    zero = jnp.zeros_like(state)
    s, ab, c = split3(s), split3(ab), split3(c + SOFTENING)
    x2 = [-2.0 * z for z in xs]
    xs, vs = [-z for z in xs], [-z for z in vs]

    def block(*rows):
        return jnp.concatenate(rows, axis=0)

    radial = block(
        vs[0], xs[0], one, s[0],
        vs[1], xs[1], none, s[1],
        vs[0], xs[0], one, none,
        zero,
        vs[2], xs[2], none, s[2],
        vs[1], xs[1], none, none,
        zero,
        vs[0], xs[0], one, none,
        zero, zero, zero, zero,
    )
    square = block(
        x2[0], void, none, ab[0],
        x2[1], void, none, ab[1],
        x2[0], void, none, none,
        one, one, one, ab[2], void, none,
        x2[2], void, none, c[0],
        x2[1], void, none, none,
        x2[2], void, none, none,
        x2[0], void, none, none,
        x2[1], void, none, none,
        x2[2], void, none, none,
        one, one, one, c[1], c[2], void,
        zero,
    )
    return jnp.concatenate([radial, square], axis=1).astype(jnp.bfloat16)


def force_kernel(cnt_ref, tgt_ref, src_ref, out_ref, dense, src_t, packed, offs):
    n_a, n_b, stars = tgt_ref.shape[0], src_ref.shape[0], src_ref.shape[2]
    per = stars // LANES
    parts = n_b * per
    f32, bf16 = jnp.float32, jnp.bfloat16
    comp = lax.broadcasted_iota(jnp.int32, (8, LANES), 0)
    lane = lax.broadcasted_iota(jnp.int32, (8, LANES), 1)

    def piece(j):
        b, p = j // per, j % per
        return src_ref[b, :, p * LANES : (p + 1) * LANES]

    top = bottom = piece(0)
    for j in range(1, parts):
        top, bottom = jnp.maximum(top, piece(j)), jnp.minimum(bottom, piece(j))
    middle = jnp.max(top, axis=1, keepdims=True) + jnp.min(bottom, axis=1, keepdims=True)
    middle = jnp.where(comp < 6, jnp.broadcast_to(0.5 * middle, (8, LANES)), 0.0)

    for j in range(parts):
        state = piece(j) - middle
        src_t[j * LANES : (j + 1) * LANES, :] = source_features(state).T.astype(bf16)
        moment = jnp.where(comp < 6, state * state[6:7], jnp.where(comp == 6, state, 0.0))
        high, mid, low = split3(moment)
        rows = jnp.concatenate([high, mid, low, jnp.zeros((8, LANES), f32)], axis=0).astype(bf16)
        packed[j, :, 0:LANES] = rows
        packed[j, :, LANES : 2 * LANES] = rows

    def compact(k, off):
        tile, shift = off // LANES, off % LANES
        rolled = pltpu.roll(tgt_ref[k], shift, 1)
        dense[tile] = jnp.where(lane >= shift, rolled, dense[tile])
        dense[tile + 1] = rolled
        offs[k] = off
        return off + cnt_ref[0, k]

    count = lax.fori_loop(0, n_a, compact, jnp.int32(0))
    tiles = (count + LANES - 1) // LANES

    def tile_step(t, _):
        state = dense[t] - middle
        pair = target_features(state)

        def products_of(c):
            left = src_t[c * SPAN * LANES : (c + 1) * SPAN * LANES, :]
            return [
                jnp.dot(left, pair[:, :LANES], preferred_element_type=f32),
                jnp.dot(left, pair[:, LANES:], preferred_element_type=f32),
            ]

        def weights_of(prod, at):
            tiles_of = [[], [], [], []]
            for g in range(8):
                pulls, twists = [], []
                for h in range(2):
                    row = slice(at + 16 * g + 8 * h, at + 16 * g + 8 * h + 8)
                    radial = prod[0][row]
                    inv = lax.rsqrt(prod[1][row])
                    inv2 = inv * inv
                    pull = inv * inv2
                    pulls.append(pull)
                    twists.append((radial * inv2) * pull)
                for s, both in enumerate((pulls, twists)):
                    full = jnp.concatenate(both, axis=0)
                    high = full.astype(bf16)
                    tiles_of[s].append(high)
                    tiles_of[2 + s].append((full - high.astype(f32)).astype(bf16))
            return [jnp.concatenate(tiles_of[s] + tiles_of[2 + s], axis=0) for s in range(2)]

        acc = [jnp.zeros((32, LANES), f32)] * 2
        groups = parts // SPAN
        ahead = [products_of(c) for c in range(AHEAD)]
        right = None
        for c in range(groups):
            if c + AHEAD < groups:
                ahead.append(products_of(c + AHEAD))
            for u in range(SPAN):
                last, right = right, weights_of(ahead[c], u * LANES)
                if last is not None:
                    acc = [
                        z + jnp.dot(packed[c * SPAN + u - 1], w, preferred_element_type=f32)
                        for z, w in zip(acc, last)
                    ]
        acc = [
            z + jnp.dot(packed[parts - 1], w, preferred_element_type=f32)
            for z, w in zip(acc, right)
        ]
        pull, twist = [z[0:8] + (z[8:16] + z[16:24]) for z in acc]
        force = pull - state * pull[6:7]
        tide = twist - state * twist[6:7]
        jerk = force[3:6] - 3.0 * tide[0:3]
        dense[t] = jnp.concatenate([force[0:3], jerk, jnp.zeros((2, LANES), f32)], axis=0)
        return 0

    lax.fori_loop(0, tiles, tile_step, 0)

    def spread(k, _):
        off = offs[k]
        tile, shift = off // LANES, off % LANES
        both = jnp.where(lane >= shift, dense[tile], dense[tile + 1])
        out_ref[k] = pltpu.roll(both, (LANES - shift) % LANES, 1)
        return 0

    lax.fori_loop(0, n_a, spread, 0)


def return_kernel(
    n_row, n_col,
    step_ref, count_ref, part_ref, pos_ref, vel_ref, acc_ref, jerk_ref, time_ref, index_ref,
    new_pos, new_vel, new_acc, new_jerk,
    inbox, send_sem, recv_sem,
):
    n_a = ROWS * n_col
    barrier = pltpu.get_barrier_semaphore()

    def greet(k, _):
        pl.semaphore_signal(barrier, inc=1, device_id=peer_a(k, n_col), device_id_type=MESH)
        return 0

    lax.fori_loop(1, n_a, greet, 0)
    stars = pos_ref.shape[1]
    clock = step_ref[0]
    span = clock - time_ref[...].reshape(1, stars)
    pos, vel, acc, jerk = pos_ref[...], vel_ref[...], acc_ref[...], jerk_ref[...]
    pred_pos, pred_vel = predict(pos, vel, acc, jerk, span)
    pick = one_hot(index_ref[...], count_ref[0, 0], stars)
    pl.semaphore_wait(barrier, n_a - 1)

    def copy(k):
        return pltpu.make_async_remote_copy(
            src_ref=part_ref.at[k], dst_ref=inbox.at[n_a - k],
            send_sem=send_sem.at[k], recv_sem=recv_sem.at[n_a - k],
            device_id=peer_a(k, n_col), device_id_type=MESH,
        )

    def start(k, _):
        copy(k).start()
        return 0

    def wait(k, _):
        copy(k).wait()
        return 0

    lax.fori_loop(1, n_a, start, 0)
    lax.fori_loop(1, n_a, wait, 0)
    total = part_ref[0]
    for k in range(1, n_a):
        total = total + inbox[k]
    comp = lax.broadcasted_iota(jnp.int32, (8, LANES), 0)
    total = jnp.where(comp < 6, total, 1.0)
    placed = lax.dot_general(
        total, pick, (((1,), (1,)), ((), ())), precision=HIGHEST,
        preferred_element_type=jnp.float32,
    )
    active = placed[6:7] > 0.5
    acc1, jerk1 = placed[0:3], placed[3:6]
    change = acc - acc1
    snap = -6.0 * change - span * (4.0 * jerk + 2.0 * jerk1)
    crack = 12.0 * change + 6.0 * span * (jerk + jerk1)
    out_pos = pred_pos + span * span * (snap / 24.0 + crack / 120.0)
    out_vel = pred_vel + span * (snap / 6.0 + crack / 24.0)
    new_pos[...] = jnp.where(active, out_pos, pos)
    new_vel[...] = jnp.where(active, out_vel, vel)
    new_acc[...] = jnp.where(active, acc1, acc)
    new_jerk[...] = jnp.where(active, jerk1, jerk)


def solution(mesh):
    n_row, n_col = mesh.shape["row"], mesh.shape["col"]
    n_a, n_b = ROWS * n_col, n_row // ROWS
    vmem = pl.BlockSpec(memory_space=pltpu.VMEM)
    smem = pl.BlockSpec(memory_space=pltpu.SMEM)
    f32 = jnp.float32

    def per_device(pos, vel, acc, jerk, mass, time, steps, index, count):
        stars = pos.shape[1]
        strength = GRAVITY / (stars * n_row * n_col)
        tgt, src, cnt = pl.pallas_call(
            functools.partial(exchange_kernel, n_row, n_col, strength),
            out_shape=(
                jax.ShapeDtypeStruct((n_a, 8, LANES), f32),
                jax.ShapeDtypeStruct((n_b, 8, stars), f32),
                jax.ShapeDtypeStruct((1, LANES), jnp.int32),
            ),
            in_specs=[smem, smem] + [vmem] * 7,
            out_specs=(vmem, vmem, vmem),
            scratch_shapes=[
                pltpu.SemaphoreType.DMA((n_a,)),
                pltpu.SemaphoreType.DMA((n_a,)),
                pltpu.SemaphoreType.DMA((n_b,)),
                pltpu.SemaphoreType.DMA((n_b,)),
            ],
            compiler_params=pltpu.CompilerParams(collective_id=0, has_side_effects=True),
            name="exchange",
        )(steps, count, pos, vel, acc, jerk, mass, time, index)
        chunks = n_b * stars // LANES
        part = pl.pallas_call(
            force_kernel,
            out_shape=jax.ShapeDtypeStruct((n_a, 8, LANES), f32),
            in_specs=[smem, vmem, vmem],
            out_specs=vmem,
            scratch_shapes=[
                pltpu.VMEM((n_a + 2, 8, LANES), f32),
                pltpu.VMEM((chunks * LANES, 96), jnp.bfloat16),
                pltpu.VMEM((chunks, 32, 2 * LANES), jnp.bfloat16),
                pltpu.SMEM((n_a,), jnp.int32),
            ],
            name="forces",
        )(cnt, tgt, src)
        return pl.pallas_call(
            functools.partial(return_kernel, n_row, n_col),
            out_shape=(jax.ShapeDtypeStruct(pos.shape, f32),) * 4,
            in_specs=[smem, smem] + [vmem] * 7,
            out_specs=(vmem,) * 4,
            scratch_shapes=[
                pltpu.VMEM((n_a, 8, LANES), f32),
                pltpu.SemaphoreType.DMA((n_a,)),
                pltpu.SemaphoreType.DMA((n_a,)),
            ],
            compiler_params=pltpu.CompilerParams(collective_id=1, has_side_effects=True),
            name="returns",
        )(steps, count, part, pos, vel, acc, jerk, time, index)

    both = ("row", "col")
    state = P(None, both)
    return jax.shard_map(
        per_device,
        mesh=mesh,
        in_specs=(state, state, state, state, P(both), P(both), P(), state, state),
        out_specs=(state, state, state, state),
        check_vma=False,
    )
```

```python
import functools

import jax
import jax.numpy as jnp
from jax import lax
from jax.experimental import pallas as pl
from jax.experimental.pallas import tpu as pltpu
from jax.sharding import PartitionSpec as P

SOFTENING = 0.0025
GRAVITY = 8.0
LANES = 128
ROWS = 2
AHEAD = 2
SPAN = 2
GRANT = 8 << 20
MESH = pl.DeviceIdType.MESH
HIGHEST = lax.Precision.HIGHEST


def predict(pos, vel, acc, jerk, elapsed):
    square = elapsed * elapsed
    pred_pos = pos + vel * elapsed + acc * (square * 0.5) + jerk * (square * elapsed / 6.0)
    pred_vel = vel + acc * elapsed + jerk * (square * 0.5)
    return pred_pos, pred_vel


def peer_a(k, n_col):
    group = ROWS * n_col
    row, col = lax.axis_index("row"), lax.axis_index("col")
    mine = (row % ROWS) * n_col + col
    other = (mine + k) % group
    return (row // ROWS) * ROWS + other // n_col, other % n_col


def peer_b(k, n_row):
    group = n_row // ROWS
    row, col = lax.axis_index("row"), lax.axis_index("col")
    return ((row // ROWS + k) % group) * ROWS + row % ROWS, col


def one_hot(index_row, count, stars):
    star = lax.broadcasted_iota(jnp.int32, (stars, LANES), 0)
    slot = lax.broadcasted_iota(jnp.int32, (stars, LANES), 1)
    return jnp.where((star == index_row) & (slot < count), 1.0, 0.0)


def exchange_kernel(
    n_row, n_col, strength,
    step_ref, count_ref, *refs,
):
    inputs, (tgt_ref, src_ref, cnt_ref), rest = refs[:7], refs[7:10], refs[10:]
    local, (load_sem, send_a, recv_a, send_b, recv_b) = rest[:7], rest[7:]
    pos_ref, vel_ref, acc_ref, jerk_ref, mass_ref, time_ref, index_ref = local
    n_a, n_b = ROWS * n_col, n_row // ROWS
    barrier = pltpu.get_barrier_semaphore()

    def greet_a(k, _):
        pl.semaphore_signal(barrier, inc=1, device_id=peer_a(k, n_col), device_id_type=MESH)
        return 0

    def greet_b(k, _):
        pl.semaphore_signal(barrier, inc=1, device_id=peer_b(k, n_row), device_id_type=MESH)
        return 0

    loads = [
        pltpu.make_async_copy(a, b, load_sem.at[i]) for i, (a, b) in enumerate(zip(inputs, local))
    ]
    for load in loads:
        load.start()
    lax.fori_loop(1, n_a, greet_a, 0)
    lax.fori_loop(1, n_b, greet_b, 0)
    for load in loads:
        load.wait()

    stars = pos_ref.shape[1]
    elapsed = step_ref[0] - time_ref[...].reshape(1, stars)
    pred_pos, pred_vel = predict(pos_ref[...], vel_ref[...], acc_ref[...], jerk_ref[...], elapsed)
    weight = mass_ref[...].reshape(1, stars) * strength
    packet = jnp.concatenate([pred_pos, pred_vel, weight, jnp.zeros_like(weight)], axis=0)
    src_ref[0] = packet
    count = count_ref[0, 0]
    chosen = jnp.dot(
        packet, one_hot(index_ref[...], LANES, stars), precision=HIGHEST,
        preferred_element_type=jnp.float32,
    )
    comp = lax.broadcasted_iota(jnp.int32, (8, LANES), 0)
    tgt_ref[0] = jnp.where(comp == 6, count.astype(jnp.float32), chosen)

    pl.semaphore_wait(barrier, n_a + n_b - 2)

    def copy_b(k):
        return pltpu.make_async_remote_copy(
            src_ref=src_ref.at[0], dst_ref=src_ref.at[n_b - k],
            send_sem=send_b.at[k], recv_sem=recv_b.at[n_b - k],
            device_id=peer_b(k, n_row), device_id_type=MESH,
        )

    def copy_a(k):
        return pltpu.make_async_remote_copy(
            src_ref=tgt_ref.at[0], dst_ref=tgt_ref.at[n_a - k],
            send_sem=send_a.at[k], recv_sem=recv_a.at[n_a - k],
            device_id=peer_a(k, n_col), device_id_type=MESH,
        )

    def start_b(k, _):
        copy_b(k).start()
        return 0

    def start_a(k, _):
        copy_a(k).start()
        return 0

    def wait_b(k, _):
        copy_b(k).wait()
        return 0

    def wait_a(k, _):
        copy_a(k).wait()
        return 0

    lax.fori_loop(1, n_b, start_b, 0)
    lax.fori_loop(1, n_a, start_a, 0)
    lax.fori_loop(1, n_a, wait_a, 0)
    lane = lax.broadcasted_iota(jnp.int32, (1, LANES), 1)
    counts = jnp.zeros((1, LANES), jnp.float32)
    for k in range(n_a):
        counts = jnp.where(lane == k, tgt_ref[k, 6:7, :], counts)
    cnt_ref[...] = counts.astype(jnp.int32)
    lax.fori_loop(1, n_b, wait_b, 0)


def split3(x):
    high = x.astype(jnp.bfloat16).astype(jnp.float32)
    rest = x - high
    mid = rest.astype(jnp.bfloat16).astype(jnp.float32)
    return high, mid, (rest - mid).astype(jnp.bfloat16).astype(jnp.float32)


def grid3(x):
    coarse = jnp.floor(x * 8.0 + 0.5) * 0.125
    rest = x - coarse
    fine = jnp.floor(rest * 4096.0 + 0.5) * (1.0 / 4096.0)
    return coarse, fine, (rest - fine).astype(jnp.bfloat16).astype(jnp.float32)


def sum3(x):
    return x[0:1] + x[1:2] + x[2:3]


def levels(state):
    xg, xm, xr = grid3(state[0:3])
    vh, vm, vl = split3(state[3:6])
    x, v = xg + xm + xr, vh + vm + vl
    scalars = [
        sum3(x * v),
        sum3(xg * xg + 2.0 * (xg * xm)),
        sum3(xm * xm + 2.0 * (xg * xr) + 2.0 * (xm * xr) + xr * xr),
    ]
    return (xg, xm, xr), (vh, vm, vl), scalars


def source_features(state):
    xs, vs, (s, ab, c) = levels(state)
    one = jnp.ones_like(state[0:1])
    none = jnp.zeros_like(one)
    s, ab, c = split3(s), split3(ab), split3(c)
    g = jnp.concatenate([xs[0], vs[0], s[0], one], axis=0)
    m = jnp.concatenate([xs[1], vs[1], s[1], none], axis=0)
    r = jnp.concatenate([xs[2], vs[2], s[2], none], axis=0)
    e = jnp.concatenate([*ab, one, none, none, none, none], axis=0)
    f = jnp.concatenate([*c, one, one, none, none, none], axis=0)
    return jnp.concatenate([g, g, m, e, g, m, m, r, r, r, f, jnp.zeros_like(f)], axis=0)


def target_features(state):
    xs, vs, (s, ab, c) = levels(state)
    one = jnp.ones_like(state[0:1])
    none = jnp.zeros_like(one)
    void = jnp.zeros_like(state[0:3])
    zero = jnp.zeros_like(state)
    s, ab, c = split3(s), split3(ab), split3(c + SOFTENING)
    x2 = [-2.0 * z for z in xs]
    xs, vs = [-z for z in xs], [-z for z in vs]

    def block(*rows):
        return jnp.concatenate(rows, axis=0)

    radial = block(
        vs[0], xs[0], one, s[0],
        vs[1], xs[1], none, s[1],
        vs[0], xs[0], one, none,
        zero,
        vs[2], xs[2], none, s[2],
        vs[1], xs[1], none, none,
        zero,
        vs[0], xs[0], one, none,
        zero, zero, zero, zero,
    )
    square = block(
        x2[0], void, none, ab[0],
        x2[1], void, none, ab[1],
        x2[0], void, none, none,
        one, one, one, ab[2], void, none,
        x2[2], void, none, c[0],
        x2[1], void, none, none,
        x2[2], void, none, none,
        x2[0], void, none, none,
        x2[1], void, none, none,
        x2[2], void, none, none,
        one, one, one, c[1], c[2], void,
        zero,
    )
    return jnp.concatenate([radial, square], axis=1).astype(jnp.bfloat16)


def force_kernel(cnt_ref, tgt_ref, src_ref, out_ref, dense, src_t, packed, offs):
    n_a, n_b, stars = tgt_ref.shape[0], src_ref.shape[0], src_ref.shape[2]
    per = stars // LANES
    parts = n_b * per
    f32, bf16 = jnp.float32, jnp.bfloat16
    comp = lax.broadcasted_iota(jnp.int32, (8, LANES), 0)
    lane = lax.broadcasted_iota(jnp.int32, (8, LANES), 1)

    def piece(j):
        b, p = j // per, j % per
        return src_ref[b, :, p * LANES : (p + 1) * LANES]

    top = bottom = piece(0)
    for j in range(1, parts):
        top, bottom = jnp.maximum(top, piece(j)), jnp.minimum(bottom, piece(j))
    middle = jnp.max(top, axis=1, keepdims=True) + jnp.min(bottom, axis=1, keepdims=True)
    middle = jnp.where(comp < 6, jnp.broadcast_to(0.5 * middle, (8, LANES)), 0.0)

    for j in range(parts):
        state = piece(j) - middle
        src_t[j * LANES : (j + 1) * LANES, :] = source_features(state).T.astype(bf16)
        moment = jnp.where(comp < 6, state * state[6:7], jnp.where(comp == 6, state, 0.0))
        high, mid, low = split3(moment)
        rows = jnp.concatenate([high, mid, low, jnp.zeros((8, LANES), f32)], axis=0).astype(bf16)
        packed[j, :, 0:LANES] = rows
        packed[j, :, LANES : 2 * LANES] = rows

    def compact(k, off):
        tile, shift = off // LANES, off % LANES
        rolled = pltpu.roll(tgt_ref[k], shift, 1)
        dense[tile] = jnp.where(lane >= shift, rolled, dense[tile])
        dense[tile + 1] = rolled
        offs[k] = off
        return off + cnt_ref[0, k]

    count = lax.fori_loop(0, n_a, compact, jnp.int32(0))
    tiles = (count + LANES - 1) // LANES

    def tile_step(t, _):
        state = dense[t] - middle
        pair = target_features(state)

        def products_of(c):
            left = src_t[c * SPAN * LANES : (c + 1) * SPAN * LANES, :]
            return [
                jnp.dot(left, pair[:, :LANES], preferred_element_type=f32),
                jnp.dot(left, pair[:, LANES:], preferred_element_type=f32),
            ]

        def weights_of(prod, at):
            tiles_of = [[], [], [], []]
            for g in range(8):
                pulls, twists = [], []
                for h in range(2):
                    row = slice(at + 16 * g + 8 * h, at + 16 * g + 8 * h + 8)
                    radial = prod[0][row]
                    inv = lax.rsqrt(prod[1][row])
                    inv2 = inv * inv
                    pull = inv * inv2
                    pulls.append(pull)
                    twists.append((radial * inv2) * pull)
                for s, both in enumerate((pulls, twists)):
                    full = jnp.concatenate(both, axis=0)
                    high = full.astype(bf16)
                    tiles_of[s].append(high)
                    tiles_of[2 + s].append((full - high.astype(f32)).astype(bf16))
            return [jnp.concatenate(tiles_of[s] + tiles_of[2 + s], axis=0) for s in range(2)]

        acc = [jnp.zeros((32, LANES), f32)] * 2
        groups = parts // SPAN
        ahead = [products_of(c) for c in range(AHEAD)]
        right = None
        for c in range(groups):
            if c + AHEAD < groups:
                ahead.append(products_of(c + AHEAD))
            for u in range(SPAN):
                last, right = right, weights_of(ahead[c], u * LANES)
                if last is not None:
                    acc = [
                        z + jnp.dot(packed[c * SPAN + u - 1], w, preferred_element_type=f32)
                        for z, w in zip(acc, last)
                    ]
        acc = [
            z + jnp.dot(packed[parts - 1], w, preferred_element_type=f32)
            for z, w in zip(acc, right)
        ]
        pull, twist = [z[0:8] + (z[8:16] + z[16:24]) for z in acc]
        force = pull - state * pull[6:7]
        tide = twist - state * twist[6:7]
        jerk = force[3:6] - 3.0 * tide[0:3]
        dense[t] = jnp.concatenate([force[0:3], jerk, jnp.zeros((2, LANES), f32)], axis=0)
        return 0

    lax.fori_loop(0, tiles, tile_step, 0)

    def spread(k, _):
        off = offs[k]
        tile, shift = off // LANES, off % LANES
        both = jnp.where(lane >= shift, dense[tile], dense[tile + 1])
        out_ref[k] = pltpu.roll(both, (LANES - shift) % LANES, 1)
        return 0

    lax.fori_loop(0, n_a, spread, 0)


def return_kernel(n_row, n_col, step_ref, count_ref, part_ref, *refs):
    inputs, outs, rest = refs[:6], refs[6:10], refs[10:]
    local, (load_sem, inbox, send_sem, recv_sem) = rest[:6], rest[6:]
    pos_ref, vel_ref, acc_ref, jerk_ref, time_ref, index_ref = local
    n_a = ROWS * n_col
    loads = [
        pltpu.make_async_copy(a, b, load_sem.at[i]) for i, (a, b) in enumerate(zip(inputs, local))
    ]
    barrier = pltpu.get_barrier_semaphore()

    def greet(k, _):
        pl.semaphore_signal(barrier, inc=1, device_id=peer_a(k, n_col), device_id_type=MESH)
        return 0

    lax.fori_loop(1, n_a, greet, 0)
    for load in loads:
        load.start()
    for load in loads:
        load.wait()
    stars = pos_ref.shape[1]
    pos, vel, acc, jerk = pos_ref[...], vel_ref[...], acc_ref[...], jerk_ref[...]
    span = step_ref[0] - time_ref[...].reshape(1, stars)
    pred_pos, pred_vel = predict(pos, vel, acc, jerk, span)
    pick = one_hot(index_ref[...], count_ref[0, 0], stars)
    pl.semaphore_wait(barrier, n_a - 1)

    def copy(k):
        return pltpu.make_async_remote_copy(
            src_ref=part_ref.at[k], dst_ref=inbox.at[n_a - k],
            send_sem=send_sem.at[k], recv_sem=recv_sem.at[n_a - k],
            device_id=peer_a(k, n_col), device_id_type=MESH,
        )

    def start(k, _):
        copy(k).start()
        return 0

    def wait(k, _):
        copy(k).wait()
        return 0

    lax.fori_loop(1, n_a, start, 0)
    lax.fori_loop(1, n_a, wait, 0)
    total = part_ref[0]
    for k in range(1, n_a):
        total = total + inbox[k]
    comp = lax.broadcasted_iota(jnp.int32, (8, LANES), 0)
    total = jnp.where(comp < 6, total, 1.0)
    placed = lax.dot_general(
        total, pick, (((1,), (1,)), ((), ())), precision=HIGHEST,
        preferred_element_type=jnp.float32,
    )
    active = placed[6:7] > 0.5
    acc1, jerk1 = placed[0:3], placed[3:6]
    change = acc - acc1
    snap = -6.0 * change - span * (4.0 * jerk + 2.0 * jerk1)
    crack = 12.0 * change + 6.0 * span * (jerk + jerk1)
    out_pos = pred_pos + span * span * (snap / 24.0 + crack / 120.0)
    out_vel = pred_vel + span * (snap / 6.0 + crack / 24.0)
    outs[0][...] = jnp.where(active, out_pos, pos)
    outs[1][...] = jnp.where(active, out_vel, vel)
    outs[2][...] = jnp.where(active, acc1, acc)
    outs[3][...] = jnp.where(active, jerk1, jerk)


def store_kernel(*refs):
    inputs, outs, sem = refs[:4], refs[4:8], refs[8]
    copies = [pltpu.make_async_copy(a, b, sem.at[i]) for i, (a, b) in enumerate(zip(inputs, outs))]
    for copy in copies:
        copy.start()
    for copy in copies:
        copy.wait()


def solution(mesh):
    n_row, n_col = mesh.shape["row"], mesh.shape["col"]
    n_a, n_b = ROWS * n_col, n_row // ROWS
    vmem = pl.BlockSpec(memory_space=pltpu.VMEM)
    smem = pl.BlockSpec(memory_space=pltpu.SMEM)
    hbm = pl.BlockSpec(memory_space=pltpu.HBM)
    f32 = jnp.float32

    def pin(x):
        return pltpu.with_memory_space_constraint(x, pltpu.HBM)

    def per_device(pos, vel, acc, jerk, mass, time, steps, index, count):
        stars = pos.shape[1]
        strength = GRAVITY / (stars * n_row * n_col)
        arrays = (pos, vel, acc, jerk, mass, time, index)
        tgt, src, cnt = pl.pallas_call(
            functools.partial(exchange_kernel, n_row, n_col, strength),
            out_shape=(
                jax.ShapeDtypeStruct((n_a, 8, LANES), f32),
                jax.ShapeDtypeStruct((n_b, 8, stars), f32),
                jax.ShapeDtypeStruct((1, LANES), jnp.int32),
            ),
            in_specs=[smem, smem] + [hbm] * 7,
            out_specs=(vmem, vmem, vmem),
            scratch_shapes=[
                *[pltpu.VMEM(x.shape, x.dtype) for x in arrays],
                pltpu.SemaphoreType.DMA((7,)),
                pltpu.SemaphoreType.DMA((n_a,)),
                pltpu.SemaphoreType.DMA((n_a,)),
                pltpu.SemaphoreType.DMA((n_b,)),
                pltpu.SemaphoreType.DMA((n_b,)),
            ],
            compiler_params=pltpu.CompilerParams(
                collective_id=0, has_side_effects=True, vmem_limit_bytes=GRANT
            ),
            name="exchange",
        )(steps, count, *[pin(x) for x in arrays])
        chunks = n_b * stars // LANES
        part = pl.pallas_call(
            force_kernel,
            out_shape=jax.ShapeDtypeStruct((n_a, 8, LANES), f32),
            in_specs=[smem, vmem, vmem],
            out_specs=vmem,
            scratch_shapes=[
                pltpu.VMEM((n_a + 2, 8, LANES), f32),
                pltpu.VMEM((chunks * LANES, 96), jnp.bfloat16),
                pltpu.VMEM((chunks, 32, 2 * LANES), jnp.bfloat16),
                pltpu.SMEM((n_a,), jnp.int32),
            ],
            compiler_params=pltpu.CompilerParams(vmem_limit_bytes=2 * GRANT),
            name="forces",
        )(cnt, tgt, src)
        arrays = (pos, vel, acc, jerk, time, index)
        news = pl.pallas_call(
            functools.partial(return_kernel, n_row, n_col),
            out_shape=(jax.ShapeDtypeStruct(pos.shape, f32),) * 4,
            in_specs=[smem, smem, vmem] + [hbm] * 6,
            out_specs=(vmem,) * 4,
            scratch_shapes=[
                *[pltpu.VMEM(x.shape, x.dtype) for x in arrays],
                pltpu.SemaphoreType.DMA((6,)),
                pltpu.VMEM((n_a, 8, LANES), f32),
                pltpu.SemaphoreType.DMA((n_a,)),
                pltpu.SemaphoreType.DMA((n_a,)),
            ],
            compiler_params=pltpu.CompilerParams(
                collective_id=1, has_side_effects=True, vmem_limit_bytes=GRANT
            ),
            name="returns",
        )(steps, count, part, *[pin(x) for x in arrays])
        return pl.pallas_call(
            store_kernel,
            out_shape=(jax.ShapeDtypeStruct(pos.shape, f32),) * 4,
            in_specs=[vmem] * 4,
            out_specs=(hbm,) * 4,
            scratch_shapes=[pltpu.SemaphoreType.DMA((4,))],
            compiler_params=pltpu.CompilerParams(vmem_limit_bytes=GRANT),
            name="store",
        )(*news)

    both = ("row", "col")
    state = P(None, both)
    return jax.shard_map(
        per_device,
        mesh=mesh,
        in_specs=(state, state, state, state, P(both), P(both), P(), state, state),
        out_specs=(state, state, state, state),
        check_vma=False,
    )
```

```python
import functools
import math

import jax
import jax.numpy as jnp
from jax import lax
from jax.experimental import pallas as pl
from jax.experimental.pallas import tpu as pltpu
from jax.sharding import PartitionSpec as P

SOFTENING = 0.0025
GRAVITY = 8.0
LANES = 128
ROWS = 2
AHEAD = 2
SPAN = 2
GRANT = 8 << 20
MESH = pl.DeviceIdType.MESH
HIGHEST = lax.Precision.HIGHEST


def predict(pos, vel, acc, jerk, elapsed):
    square = elapsed * elapsed
    pred_pos = pos + vel * elapsed + acc * (square * 0.5) + jerk * (square * elapsed / 6.0)
    pred_vel = vel + acc * elapsed + jerk * (square * 0.5)
    return pred_pos, pred_vel


def near(step, size):
    return min(step, size - step)


def plane_peers(n_col):
    side = math.isqrt(n_col)
    row, col = lax.axis_index("row"), lax.axis_index("col")
    x, y, core = lax.div(col, side), lax.rem(col, side), lax.rem(row, ROWS)
    xs = [lax.rem(x + i, side) * side for i in range(side)]
    ys = [lax.rem(y + i, side) for i in range(side)]
    rows = [row - core + lax.rem(core + i, ROWS) for i in range(ROWS)]
    peers = []
    for i in range(ROWS):
        for j in range(side):
            for k in range(side):
                slot = (i * side + j) * side + k
                back = ((-i % ROWS) * side + (-j % side)) * side + (-k % side)
                far = near(j, side) + near(k, side)
                peers.append((far, slot, back, (rows[i], xs[j] + ys[k])))
    return sorted(peers[1:], key=lambda peer: -peer[0])


def line_peers(n_row):
    size = n_row // ROWS
    row, col = lax.axis_index("row"), lax.axis_index("col")
    place, core = lax.div(row, ROWS), lax.rem(row, ROWS)
    peers = [
        (near(i, size), i, size - i, (lax.rem(place + i, size) * ROWS + core, col))
        for i in range(1, size)
    ]
    return sorted(peers, key=lambda peer: -peer[0])


def greet(peers):
    barrier = pltpu.get_barrier_semaphore()
    for _, _, _, device in sorted(peers, key=lambda peer: -peer[0]):
        pl.semaphore_signal(barrier, inc=1, device_id=device, device_id_type=MESH)


def one_hot(index_row, count, stars):
    star = lax.broadcasted_iota(jnp.int32, (stars, LANES), 0)
    slot = lax.broadcasted_iota(jnp.int32, (stars, LANES), 1)
    return jnp.where((star == index_row) & (slot < count), 1.0, 0.0)


def exchange_kernel(
    n_row, n_col, strength,
    step_ref, count_ref, *refs,
):
    inputs, (tgt_ref, src_ref, cnt_ref), rest = refs[:7], refs[7:10], refs[10:]
    local, (load_sem, send_a, recv_a, send_b, recv_b) = rest[:7], rest[7:]
    pos_ref, vel_ref, acc_ref, jerk_ref, mass_ref, time_ref, index_ref = local
    n_a, n_b = ROWS * n_col, n_row // ROWS
    plane, line = plane_peers(n_col), line_peers(n_row)
    loads = [
        pltpu.make_async_copy(a, b, load_sem.at[i]) for i, (a, b) in enumerate(zip(inputs, local))
    ]
    for load in loads:
        load.start()
    greet(plane + line)
    for load in loads:
        load.wait()

    stars = pos_ref.shape[1]
    elapsed = step_ref[0] - time_ref[...].reshape(1, stars)
    pred_pos, pred_vel = predict(pos_ref[...], vel_ref[...], acc_ref[...], jerk_ref[...], elapsed)
    weight = mass_ref[...].reshape(1, stars) * strength
    packet = jnp.concatenate([pred_pos, pred_vel, weight, jnp.zeros_like(weight)], axis=0)
    src_ref[0] = packet
    count = count_ref[0, 0]
    chosen = jnp.dot(
        packet, one_hot(index_ref[...], LANES, stars), precision=HIGHEST,
        preferred_element_type=jnp.float32,
    )
    comp = lax.broadcasted_iota(jnp.int32, (8, LANES), 0)
    tgt_ref[0] = jnp.where(comp == 6, count.astype(jnp.float32), chosen)

    pl.semaphore_wait(pltpu.get_barrier_semaphore(), n_a + n_b - 2)
    far = [
        pltpu.make_async_remote_copy(
            src_ref=src_ref.at[0], dst_ref=src_ref.at[back],
            send_sem=send_b.at[slot], recv_sem=recv_b.at[back],
            device_id=device, device_id_type=MESH,
        )
        for _, slot, back, device in line
    ]
    wide = [
        pltpu.make_async_remote_copy(
            src_ref=tgt_ref.at[0], dst_ref=tgt_ref.at[back],
            send_sem=send_a.at[slot], recv_sem=recv_a.at[back],
            device_id=device, device_id_type=MESH,
        )
        for _, slot, back, device in plane
    ]
    for copy in far + wide:
        copy.start()
    for copy in wide:
        copy.wait()
    lane = lax.broadcasted_iota(jnp.int32, (1, LANES), 1)
    counts = jnp.zeros((1, LANES), jnp.float32)
    for k in range(n_a):
        counts = jnp.where(lane == k, tgt_ref[k, 6:7, :], counts)
    cnt_ref[...] = counts.astype(jnp.int32)
    for copy in far:
        copy.wait()


def split3(x):
    high = x.astype(jnp.bfloat16).astype(jnp.float32)
    rest = x - high
    mid = rest.astype(jnp.bfloat16).astype(jnp.float32)
    return high, mid, (rest - mid).astype(jnp.bfloat16).astype(jnp.float32)


def grid3(x):
    coarse = jnp.floor(x * 8.0 + 0.5) * 0.125
    rest = x - coarse
    fine = jnp.floor(rest * 4096.0 + 0.5) * (1.0 / 4096.0)
    return coarse, fine, (rest - fine).astype(jnp.bfloat16).astype(jnp.float32)


def sum3(x):
    return x[0:1] + x[1:2] + x[2:3]


def levels(state):
    xg, xm, xr = grid3(state[0:3])
    vh, vm, vl = split3(state[3:6])
    x, v = xg + xm + xr, vh + vm + vl
    scalars = [
        sum3(x * v),
        sum3(xg * xg + 2.0 * (xg * xm)),
        sum3(xm * xm + 2.0 * (xg * xr) + 2.0 * (xm * xr) + xr * xr),
    ]
    return (xg, xm, xr), (vh, vm, vl), scalars


def source_features(state):
    xs, vs, (s, ab, c) = levels(state)
    one = jnp.ones_like(state[0:1])
    none = jnp.zeros_like(one)
    s, ab, c = split3(s), split3(ab), split3(c)
    g = jnp.concatenate([xs[0], vs[0], s[0], one], axis=0)
    m = jnp.concatenate([xs[1], vs[1], s[1], none], axis=0)
    r = jnp.concatenate([xs[2], vs[2], s[2], none], axis=0)
    e = jnp.concatenate([*ab, one, none, none, none, none], axis=0)
    f = jnp.concatenate([*c, one, one, none, none, none], axis=0)
    return jnp.concatenate([g, g, m, e, g, m, m, r, r, r, f, jnp.zeros_like(f)], axis=0)


def target_features(state):
    xs, vs, (s, ab, c) = levels(state)
    one = jnp.ones_like(state[0:1])
    none = jnp.zeros_like(one)
    void = jnp.zeros_like(state[0:3])
    zero = jnp.zeros_like(state)
    s, ab, c = split3(s), split3(ab), split3(c + SOFTENING)
    x2 = [-2.0 * z for z in xs]
    xs, vs = [-z for z in xs], [-z for z in vs]

    def block(*rows):
        return jnp.concatenate(rows, axis=0)

    radial = block(
        vs[0], xs[0], one, s[0],
        vs[1], xs[1], none, s[1],
        vs[0], xs[0], one, none,
        zero,
        vs[2], xs[2], none, s[2],
        vs[1], xs[1], none, none,
        zero,
        vs[0], xs[0], one, none,
        zero, zero, zero, zero,
    )
    square = block(
        x2[0], void, none, ab[0],
        x2[1], void, none, ab[1],
        x2[0], void, none, none,
        one, one, one, ab[2], void, none,
        x2[2], void, none, c[0],
        x2[1], void, none, none,
        x2[2], void, none, none,
        x2[0], void, none, none,
        x2[1], void, none, none,
        x2[2], void, none, none,
        one, one, one, c[1], c[2], void,
        zero,
    )
    return jnp.concatenate([radial, square], axis=1).astype(jnp.bfloat16)


def force_kernel(cnt_ref, tgt_ref, src_ref, out_ref, dense, src_t, packed, offs):
    n_a, n_b, stars = tgt_ref.shape[0], src_ref.shape[0], src_ref.shape[2]
    per = stars // LANES
    parts = n_b * per
    f32, bf16 = jnp.float32, jnp.bfloat16
    comp = lax.broadcasted_iota(jnp.int32, (8, LANES), 0)
    lane = lax.broadcasted_iota(jnp.int32, (8, LANES), 1)

    def piece(j):
        b, p = j // per, j % per
        return src_ref[b, :, p * LANES : (p + 1) * LANES]

    top = bottom = piece(0)
    for j in range(1, parts):
        top, bottom = jnp.maximum(top, piece(j)), jnp.minimum(bottom, piece(j))
    middle = jnp.max(top, axis=1, keepdims=True) + jnp.min(bottom, axis=1, keepdims=True)
    middle = jnp.where(comp < 6, jnp.broadcast_to(0.5 * middle, (8, LANES)), 0.0)

    for j in range(parts):
        state = piece(j) - middle
        src_t[j * LANES : (j + 1) * LANES, :] = source_features(state).T.astype(bf16)
        moment = jnp.where(comp < 6, state * state[6:7], jnp.where(comp == 6, state, 0.0))
        high, mid, low = split3(moment)
        rows = jnp.concatenate([high, mid, low, jnp.zeros((8, LANES), f32)], axis=0).astype(bf16)
        packed[j, :, 0:LANES] = rows
        packed[j, :, LANES : 2 * LANES] = rows

    def compact(k, off):
        tile, shift = off // LANES, off % LANES
        rolled = pltpu.roll(tgt_ref[k], shift, 1)
        dense[tile] = jnp.where(lane >= shift, rolled, dense[tile])
        dense[tile + 1] = rolled
        offs[k] = off
        return off + cnt_ref[0, k]

    count = lax.fori_loop(0, n_a, compact, jnp.int32(0))
    tiles = (count + LANES - 1) // LANES

    def tile_step(t, _):
        state = dense[t] - middle
        pair = target_features(state)

        def products_of(c):
            left = src_t[c * SPAN * LANES : (c + 1) * SPAN * LANES, :]
            return [
                jnp.dot(left, pair[:, :LANES], preferred_element_type=f32),
                jnp.dot(left, pair[:, LANES:], preferred_element_type=f32),
            ]

        def weights_of(prod, at):
            tiles_of = [[], [], [], []]
            for g in range(8):
                pulls, twists = [], []
                for h in range(2):
                    row = slice(at + 16 * g + 8 * h, at + 16 * g + 8 * h + 8)
                    radial = prod[0][row]
                    inv = lax.rsqrt(prod[1][row])
                    inv2 = inv * inv
                    pull = inv * inv2
                    pulls.append(pull)
                    twists.append((radial * inv2) * pull)
                for s, both in enumerate((pulls, twists)):
                    full = jnp.concatenate(both, axis=0)
                    high = full.astype(bf16)
                    tiles_of[s].append(high)
                    tiles_of[2 + s].append((full - high.astype(f32)).astype(bf16))
            return [jnp.concatenate(tiles_of[s] + tiles_of[2 + s], axis=0) for s in range(2)]

        acc = [jnp.zeros((32, LANES), f32)] * 2
        groups = parts // SPAN
        ahead = [products_of(c) for c in range(AHEAD)]
        right = None
        for c in range(groups):
            if c + AHEAD < groups:
                ahead.append(products_of(c + AHEAD))
            for u in range(SPAN):
                last, right = right, weights_of(ahead[c], u * LANES)
                if last is not None:
                    acc = [
                        z + jnp.dot(packed[c * SPAN + u - 1], w, preferred_element_type=f32)
                        for z, w in zip(acc, last)
                    ]
        acc = [
            z + jnp.dot(packed[parts - 1], w, preferred_element_type=f32)
            for z, w in zip(acc, right)
        ]
        pull, twist = [z[0:8] + (z[8:16] + z[16:24]) for z in acc]
        force = pull - state * pull[6:7]
        tide = twist - state * twist[6:7]
        jerk = force[3:6] - 3.0 * tide[0:3]
        dense[t] = jnp.concatenate([force[0:3], jerk, jnp.zeros((2, LANES), f32)], axis=0)
        return 0

    lax.fori_loop(0, tiles, tile_step, 0)

    def spread(k, _):
        off = offs[k]
        tile, shift = off // LANES, off % LANES
        both = jnp.where(lane >= shift, dense[tile], dense[tile + 1])
        out_ref[k] = pltpu.roll(both, (LANES - shift) % LANES, 1)
        return 0

    lax.fori_loop(0, n_a, spread, 0)


def return_kernel(n_row, n_col, step_ref, count_ref, part_ref, *refs):
    inputs, outs, rest = refs[:6], refs[6:10], refs[10:]
    local, (load_sem, inbox, send_sem, recv_sem) = rest[:6], rest[6:]
    pos_ref, vel_ref, acc_ref, jerk_ref, time_ref, index_ref = local
    n_a = ROWS * n_col
    loads = [
        pltpu.make_async_copy(a, b, load_sem.at[i]) for i, (a, b) in enumerate(zip(inputs, local))
    ]
    peers = plane_peers(n_col)
    greet(peers)
    for load in loads:
        load.start()
    for load in loads:
        load.wait()
    stars = pos_ref.shape[1]
    pos, vel, acc, jerk = pos_ref[...], vel_ref[...], acc_ref[...], jerk_ref[...]
    span = step_ref[0] - time_ref[...].reshape(1, stars)
    pred_pos, pred_vel = predict(pos, vel, acc, jerk, span)
    pick = one_hot(index_ref[...], count_ref[0, 0], stars)
    pl.semaphore_wait(pltpu.get_barrier_semaphore(), n_a - 1)
    copies = [
        pltpu.make_async_remote_copy(
            src_ref=part_ref.at[slot], dst_ref=inbox.at[back],
            send_sem=send_sem.at[slot], recv_sem=recv_sem.at[back],
            device_id=device, device_id_type=MESH,
        )
        for _, slot, back, device in peers
    ]
    for copy in copies:
        copy.start()
    for copy in copies:
        copy.wait()
    total = part_ref[0]
    for k in range(1, n_a):
        total = total + inbox[k]
    comp = lax.broadcasted_iota(jnp.int32, (8, LANES), 0)
    total = jnp.where(comp < 6, total, 1.0)
    placed = lax.dot_general(
        total, pick, (((1,), (1,)), ((), ())), precision=HIGHEST,
        preferred_element_type=jnp.float32,
    )
    active = placed[6:7] > 0.5
    acc1, jerk1 = placed[0:3], placed[3:6]
    change = acc - acc1
    snap = -6.0 * change - span * (4.0 * jerk + 2.0 * jerk1)
    crack = 12.0 * change + 6.0 * span * (jerk + jerk1)
    out_pos = pred_pos + span * span * (snap / 24.0 + crack / 120.0)
    out_vel = pred_vel + span * (snap / 6.0 + crack / 24.0)
    outs[0][...] = jnp.where(active, out_pos, pos)
    outs[1][...] = jnp.where(active, out_vel, vel)
    outs[2][...] = jnp.where(active, acc1, acc)
    outs[3][...] = jnp.where(active, jerk1, jerk)


def store_kernel(*refs):
    inputs, outs, sem = refs[:4], refs[4:8], refs[8]
    copies = [pltpu.make_async_copy(a, b, sem.at[i]) for i, (a, b) in enumerate(zip(inputs, outs))]
    for copy in copies:
        copy.start()
    for copy in copies:
        copy.wait()


def solution(mesh):
    n_row, n_col = mesh.shape["row"], mesh.shape["col"]
    n_a, n_b = ROWS * n_col, n_row // ROWS
    vmem = pl.BlockSpec(memory_space=pltpu.VMEM)
    smem = pl.BlockSpec(memory_space=pltpu.SMEM)
    hbm = pl.BlockSpec(memory_space=pltpu.HBM)
    f32 = jnp.float32

    def pin(x):
        return pltpu.with_memory_space_constraint(x, pltpu.HBM)

    def per_device(pos, vel, acc, jerk, mass, time, steps, index, count):
        stars = pos.shape[1]
        strength = GRAVITY / (stars * n_row * n_col)
        arrays = (pos, vel, acc, jerk, mass, time, index)
        tgt, src, cnt = pl.pallas_call(
            functools.partial(exchange_kernel, n_row, n_col, strength),
            out_shape=(
                jax.ShapeDtypeStruct((n_a, 8, LANES), f32),
                jax.ShapeDtypeStruct((n_b, 8, stars), f32),
                jax.ShapeDtypeStruct((1, LANES), jnp.int32),
            ),
            in_specs=[smem, smem] + [hbm] * 7,
            out_specs=(vmem, vmem, vmem),
            scratch_shapes=[
                *[pltpu.VMEM(x.shape, x.dtype) for x in arrays],
                pltpu.SemaphoreType.DMA((7,)),
                pltpu.SemaphoreType.DMA((n_a,)),
                pltpu.SemaphoreType.DMA((n_a,)),
                pltpu.SemaphoreType.DMA((n_b,)),
                pltpu.SemaphoreType.DMA((n_b,)),
            ],
            compiler_params=pltpu.CompilerParams(
                collective_id=0, has_side_effects=True, vmem_limit_bytes=GRANT
            ),
            name="exchange",
        )(steps, count, *[pin(x) for x in arrays])
        chunks = n_b * stars // LANES
        part = pl.pallas_call(
            force_kernel,
            out_shape=jax.ShapeDtypeStruct((n_a, 8, LANES), f32),
            in_specs=[smem, vmem, vmem],
            out_specs=vmem,
            scratch_shapes=[
                pltpu.VMEM((n_a + 2, 8, LANES), f32),
                pltpu.VMEM((chunks * LANES, 96), jnp.bfloat16),
                pltpu.VMEM((chunks, 32, 2 * LANES), jnp.bfloat16),
                pltpu.SMEM((n_a,), jnp.int32),
            ],
            compiler_params=pltpu.CompilerParams(vmem_limit_bytes=2 * GRANT),
            name="forces",
        )(cnt, tgt, src)
        arrays = (pos, vel, acc, jerk, time, index)
        news = pl.pallas_call(
            functools.partial(return_kernel, n_row, n_col),
            out_shape=(jax.ShapeDtypeStruct(pos.shape, f32),) * 4,
            in_specs=[smem, smem, vmem] + [hbm] * 6,
            out_specs=(vmem,) * 4,
            scratch_shapes=[
                *[pltpu.VMEM(x.shape, x.dtype) for x in arrays],
                pltpu.SemaphoreType.DMA((6,)),
                pltpu.VMEM((n_a, 8, LANES), f32),
                pltpu.SemaphoreType.DMA((n_a,)),
                pltpu.SemaphoreType.DMA((n_a,)),
            ],
            compiler_params=pltpu.CompilerParams(
                collective_id=1, has_side_effects=True, vmem_limit_bytes=GRANT
            ),
            name="returns",
        )(steps, count, part, *[pin(x) for x in arrays])
        return pl.pallas_call(
            store_kernel,
            out_shape=(jax.ShapeDtypeStruct(pos.shape, f32),) * 4,
            in_specs=[vmem] * 4,
            out_specs=(hbm,) * 4,
            scratch_shapes=[pltpu.SemaphoreType.DMA((4,))],
            compiler_params=pltpu.CompilerParams(vmem_limit_bytes=GRANT),
            name="store",
        )(*news)

    both = ("row", "col")
    state = P(None, both)
    return jax.shard_map(
        per_device,
        mesh=mesh,
        in_specs=(state, state, state, state, P(both), P(both), P(), state, state),
        out_specs=(state, state, state, state),
        check_vma=False,
    )
```

```python
import functools
import math

import jax
import jax.numpy as jnp
from jax import lax
from jax.experimental import pallas as pl
from jax.experimental.pallas import tpu as pltpu
from jax.sharding import PartitionSpec as P

SOFTENING = 0.0025
GRAVITY = 8.0
LANES = 128
ROWS = 2
AHEAD = 2
SPAN = 2
GRANT = 8 << 20
MESH = pl.DeviceIdType.MESH
HIGHEST = lax.Precision.HIGHEST


def predict(pos, vel, acc, jerk, elapsed):
    square = elapsed * elapsed
    pred_pos = pos + vel * elapsed + acc * (square * 0.5) + jerk * (square * elapsed / 6.0)
    pred_vel = vel + acc * elapsed + jerk * (square * 0.5)
    return pred_pos, pred_vel


def near(step, size):
    return min(step, size - step)


def plane_peers(n_col):
    side = math.isqrt(n_col)
    row, col = lax.axis_index("row"), lax.axis_index("col")
    x, y, core = lax.div(col, side), lax.rem(col, side), lax.rem(row, ROWS)
    xs = [lax.rem(x + i, side) * side for i in range(side)]
    ys = [lax.rem(y + i, side) for i in range(side)]
    rows = [row - core + lax.rem(core + i, ROWS) for i in range(ROWS)]
    peers = []
    for i in range(ROWS):
        for j in range(side):
            for k in range(side):
                slot = (i * side + j) * side + k
                back = ((-i % ROWS) * side + (-j % side)) * side + (-k % side)
                far = near(j, side) + near(k, side)
                peers.append((far, slot, back, (rows[i], xs[j] + ys[k])))
    return sorted(peers[1:], key=lambda peer: -peer[0])


def line_peers(n_row):
    size = n_row // ROWS
    row, col = lax.axis_index("row"), lax.axis_index("col")
    place, core = lax.div(row, ROWS), lax.rem(row, ROWS)
    peers = [
        (near(i, size), i, size - i, (lax.rem(place + i, size) * ROWS + core, col))
        for i in range(1, size)
    ]
    return sorted(peers, key=lambda peer: -peer[0])


def greet(peers):
    barrier = pltpu.get_barrier_semaphore()
    for _, _, _, device in sorted(peers, key=lambda peer: -peer[0]):
        pl.semaphore_signal(barrier, inc=1, device_id=device, device_id_type=MESH)


def one_hot(index_row, count, stars):
    star = lax.broadcasted_iota(jnp.int32, (stars, LANES), 0)
    slot = lax.broadcasted_iota(jnp.int32, (stars, LANES), 1)
    return jnp.where((star == index_row) & (slot < count), 1.0, 0.0)


def exchange_kernel(
    n_row, n_col, strength,
    step_ref, count_ref, *refs,
):
    inputs, (tgt_ref, src_ref, cnt_ref), rest = refs[:7], refs[7:10], refs[10:]
    local, (load_sem, send_a, recv_a, send_b, recv_b) = rest[:7], rest[7:]
    pos_ref, vel_ref, acc_ref, jerk_ref, mass_ref, time_ref, index_ref = local
    n_a, n_b = ROWS * n_col, n_row // ROWS
    plane, line = plane_peers(n_col), line_peers(n_row)
    loads = [
        pltpu.make_async_copy(a, b, load_sem.at[i]) for i, (a, b) in enumerate(zip(inputs, local))
    ]
    for load in loads:
        load.start()
    greet(plane + line)
    for load in loads:
        load.wait()

    stars = pos_ref.shape[1]
    elapsed = step_ref[0] - time_ref[...].reshape(1, stars)
    pred_pos, pred_vel = predict(pos_ref[...], vel_ref[...], acc_ref[...], jerk_ref[...], elapsed)
    weight = mass_ref[...].reshape(1, stars) * strength
    packet = jnp.concatenate([pred_pos, pred_vel, weight, jnp.zeros_like(weight)], axis=0)
    src_ref[0] = packet
    count = count_ref[0, 0]
    chosen = jnp.dot(
        packet, one_hot(index_ref[...], LANES, stars), precision=HIGHEST,
        preferred_element_type=jnp.float32,
    )
    comp = lax.broadcasted_iota(jnp.int32, (8, LANES), 0)
    tgt_ref[0] = jnp.where(comp == 6, count.astype(jnp.float32), chosen)

    pl.semaphore_wait(pltpu.get_barrier_semaphore(), n_a + n_b - 2)
    far = [
        pltpu.make_async_remote_copy(
            src_ref=src_ref.at[0, 0:7], dst_ref=src_ref.at[back, 0:7],
            send_sem=send_b.at[slot], recv_sem=recv_b.at[back],
            device_id=device, device_id_type=MESH,
        )
        for _, slot, back, device in line
    ]
    wide = [
        pltpu.make_async_remote_copy(
            src_ref=tgt_ref.at[0, 0:7], dst_ref=tgt_ref.at[back, 0:7],
            send_sem=send_a.at[slot], recv_sem=recv_a.at[back],
            device_id=device, device_id_type=MESH,
        )
        for _, slot, back, device in plane
    ]
    for copy in far + wide:
        copy.start()
    for copy in wide:
        copy.wait()
    lane = lax.broadcasted_iota(jnp.int32, (1, LANES), 1)
    counts = jnp.zeros((1, LANES), jnp.float32)
    for k in range(n_a):
        counts = jnp.where(lane == k, tgt_ref[k, 6:7, :], counts)
    cnt_ref[...] = counts.astype(jnp.int32)
    for copy in far:
        copy.wait()


def split3(x):
    high = x.astype(jnp.bfloat16).astype(jnp.float32)
    rest = x - high
    mid = rest.astype(jnp.bfloat16).astype(jnp.float32)
    return high, mid, (rest - mid).astype(jnp.bfloat16).astype(jnp.float32)


def grid3(x):
    coarse = jnp.floor(x * 8.0 + 0.5) * 0.125
    rest = x - coarse
    fine = jnp.floor(rest * 4096.0 + 0.5) * (1.0 / 4096.0)
    return coarse, fine, (rest - fine).astype(jnp.bfloat16).astype(jnp.float32)


def sum3(x):
    return x[0:1] + x[1:2] + x[2:3]


def levels(state):
    xg, xm, xr = grid3(state[0:3])
    vh, vm, vl = split3(state[3:6])
    x, v = xg + xm + xr, vh + vm + vl
    scalars = [
        sum3(x * v),
        sum3(xg * xg + 2.0 * (xg * xm)),
        sum3(xm * xm + 2.0 * (xg * xr) + 2.0 * (xm * xr) + xr * xr),
    ]
    return (xg, xm, xr), (vh, vm, vl), scalars


def source_features(state):
    xs, vs, (s, ab, c) = levels(state)
    one = jnp.ones_like(state[0:1])
    none = jnp.zeros_like(one)
    s, ab, c = split3(s), split3(ab), split3(c)
    g = jnp.concatenate([xs[0], vs[0], s[0], one], axis=0)
    m = jnp.concatenate([xs[1], vs[1], s[1], none], axis=0)
    r = jnp.concatenate([xs[2], vs[2], s[2], none], axis=0)
    e = jnp.concatenate([*ab, one, none, none, none, none], axis=0)
    f = jnp.concatenate([*c, one, one, none, none, none], axis=0)
    return jnp.concatenate([g, g, m, e, g, m, m, r, r, r, f, jnp.zeros_like(f)], axis=0)


def target_features(state):
    xs, vs, (s, ab, c) = levels(state)
    one = jnp.ones_like(state[0:1])
    none = jnp.zeros_like(one)
    void = jnp.zeros_like(state[0:3])
    zero = jnp.zeros_like(state)
    s, ab, c = split3(s), split3(ab), split3(c + SOFTENING)
    x2 = [-2.0 * z for z in xs]
    xs, vs = [-z for z in xs], [-z for z in vs]

    def block(*rows):
        return jnp.concatenate(rows, axis=0)

    radial = block(
        vs[0], xs[0], one, s[0],
        vs[1], xs[1], none, s[1],
        vs[0], xs[0], one, none,
        zero,
        vs[2], xs[2], none, s[2],
        vs[1], xs[1], none, none,
        zero,
        vs[0], xs[0], one, none,
        zero, zero, zero, zero,
    )
    square = block(
        x2[0], void, none, ab[0],
        x2[1], void, none, ab[1],
        x2[0], void, none, none,
        one, one, one, ab[2], void, none,
        x2[2], void, none, c[0],
        x2[1], void, none, none,
        x2[2], void, none, none,
        x2[0], void, none, none,
        x2[1], void, none, none,
        x2[2], void, none, none,
        one, one, one, c[1], c[2], void,
        zero,
    )
    return jnp.concatenate([radial, square], axis=1).astype(jnp.bfloat16)


def force_kernel(cnt_ref, tgt_ref, src_ref, out_ref, dense, src_t, packed):
    n_a, n_b, stars = tgt_ref.shape[0], src_ref.shape[0], src_ref.shape[2]
    per = stars // LANES
    parts = n_b * per
    f32, bf16 = jnp.float32, jnp.bfloat16
    comp = lax.broadcasted_iota(jnp.int32, (8, LANES), 0)
    lane = lax.broadcasted_iota(jnp.int32, (8, LANES), 1)

    def piece(j):
        b, p = j // per, j % per
        return src_ref[b, :, p * LANES : (p + 1) * LANES]

    top = bottom = piece(0)
    for j in range(1, parts):
        top, bottom = jnp.maximum(top, piece(j)), jnp.minimum(bottom, piece(j))
    middle = jnp.max(top, axis=1, keepdims=True) + jnp.min(bottom, axis=1, keepdims=True)
    middle = jnp.where(comp < 6, jnp.broadcast_to(0.5 * middle, (8, LANES)), 0.0)

    for j in range(parts):
        state = piece(j) - middle
        src_t[j * LANES : (j + 1) * LANES, :] = source_features(state).T.astype(bf16)
        moment = jnp.where(comp < 6, state * state[6:7], jnp.where(comp == 6, state, 0.0))
        high, mid, low = split3(moment)
        rows = jnp.concatenate([high, mid, low, jnp.zeros((8, LANES), f32)], axis=0).astype(bf16)
        packed[j, :, 0:LANES] = rows
        packed[j, :, LANES : 2 * LANES] = rows

    count = jnp.int32(0)
    front = tgt_ref[0]
    starts = []
    for k in range(n_a):
        starts.append(count)
        tile, shift = lax.div(count, LANES), lax.rem(count, LANES)
        rolled = pltpu.roll(tgt_ref[k], shift, 1)
        merged = jnp.where(lane >= shift, rolled, front)
        dense[tile] = merged
        dense[tile + 1] = rolled
        count = count + cnt_ref[0, k]
        front = jnp.where(lax.div(count, LANES) == tile, merged, rolled)
    tiles = (count + LANES - 1) // LANES

    def tile_step(t, _):
        state = dense[t] - middle
        pair = target_features(state)

        def products_of(c):
            left = src_t[c * SPAN * LANES : (c + 1) * SPAN * LANES, :]
            return [
                jnp.dot(left, pair[:, :LANES], preferred_element_type=f32),
                jnp.dot(left, pair[:, LANES:], preferred_element_type=f32),
            ]

        def weights_of(prod, at):
            tiles_of = [[], [], [], []]
            for g in range(8):
                pulls, twists = [], []
                for h in range(2):
                    row = slice(at + 16 * g + 8 * h, at + 16 * g + 8 * h + 8)
                    radial = prod[0][row]
                    inv = lax.rsqrt(prod[1][row])
                    inv2 = inv * inv
                    pull = inv * inv2
                    pulls.append(pull)
                    twists.append((radial * inv2) * pull)
                for s, both in enumerate((pulls, twists)):
                    full = jnp.concatenate(both, axis=0)
                    high = full.astype(bf16)
                    tiles_of[s].append(high)
                    tiles_of[2 + s].append((full - high.astype(f32)).astype(bf16))
            return [jnp.concatenate(tiles_of[s] + tiles_of[2 + s], axis=0) for s in range(2)]

        acc = [jnp.zeros((32, LANES), f32)] * 2
        groups = parts // SPAN
        ahead = [products_of(c) for c in range(AHEAD)]
        right = None
        for c in range(groups):
            if c + AHEAD < groups:
                ahead.append(products_of(c + AHEAD))
            for u in range(SPAN):
                last, right = right, weights_of(ahead[c], u * LANES)
                if last is not None:
                    acc = [
                        z + jnp.dot(packed[c * SPAN + u - 1], w, preferred_element_type=f32)
                        for z, w in zip(acc, last)
                    ]
        acc = [
            z + jnp.dot(packed[parts - 1], w, preferred_element_type=f32)
            for z, w in zip(acc, right)
        ]
        pull, twist = [z[0:8] + (z[8:16] + z[16:24]) for z in acc]
        force = pull - state * pull[6:7]
        tide = twist - state * twist[6:7]
        jerk = force[3:6] - 3.0 * tide[0:3]
        dense[t] = jnp.concatenate([force[0:3], jerk, jnp.zeros((2, LANES), f32)], axis=0)
        return 0

    lax.fori_loop(0, tiles, tile_step, 0)

    for k in range(n_a):
        tile, shift = lax.div(starts[k], LANES), lax.rem(starts[k], LANES)
        both = jnp.where(lane >= shift, dense[tile], dense[tile + 1])
        out_ref[k] = pltpu.roll(both, lax.rem(LANES - shift, LANES), 1)


def return_kernel(n_row, n_col, step_ref, count_ref, part_ref, *refs):
    inputs, outs, rest = refs[:6], refs[6:10], refs[10:]
    local, (load_sem, inbox, send_sem, recv_sem) = rest[:6], rest[6:]
    pos_ref, vel_ref, acc_ref, jerk_ref, time_ref, index_ref = local
    n_a = ROWS * n_col
    loads = [
        pltpu.make_async_copy(a, b, load_sem.at[i]) for i, (a, b) in enumerate(zip(inputs, local))
    ]
    peers = plane_peers(n_col)
    greet(peers)
    for load in loads:
        load.start()
    for load in loads:
        load.wait()
    stars = pos_ref.shape[1]
    pos, vel, acc, jerk = pos_ref[...], vel_ref[...], acc_ref[...], jerk_ref[...]
    span = step_ref[0] - time_ref[...].reshape(1, stars)
    pred_pos, pred_vel = predict(pos, vel, acc, jerk, span)
    pick = one_hot(index_ref[...], count_ref[0, 0], stars)
    pl.semaphore_wait(pltpu.get_barrier_semaphore(), n_a - 1)
    copies = [
        pltpu.make_async_remote_copy(
            src_ref=part_ref.at[slot, 0:6], dst_ref=inbox.at[back, 0:6],
            send_sem=send_sem.at[slot], recv_sem=recv_sem.at[back],
            device_id=device, device_id_type=MESH,
        )
        for _, slot, back, device in peers
    ]
    for copy in copies:
        copy.start()
    for copy in copies:
        copy.wait()
    total = part_ref[0]
    for k in range(1, n_a):
        total = total + inbox[k]
    comp = lax.broadcasted_iota(jnp.int32, (8, LANES), 0)
    total = jnp.where(comp < 6, total, 1.0)
    placed = lax.dot_general(
        total, pick, (((1,), (1,)), ((), ())), precision=HIGHEST,
        preferred_element_type=jnp.float32,
    )
    active = placed[6:7] > 0.5
    acc1, jerk1 = placed[0:3], placed[3:6]
    change = acc - acc1
    snap = -6.0 * change - span * (4.0 * jerk + 2.0 * jerk1)
    crack = 12.0 * change + 6.0 * span * (jerk + jerk1)
    out_pos = pred_pos + span * span * (snap / 24.0 + crack / 120.0)
    out_vel = pred_vel + span * (snap / 6.0 + crack / 24.0)
    outs[0][...] = jnp.where(active, out_pos, pos)
    outs[1][...] = jnp.where(active, out_vel, vel)
    outs[2][...] = jnp.where(active, acc1, acc)
    outs[3][...] = jnp.where(active, jerk1, jerk)


def store_kernel(*refs):
    inputs, outs, sem = refs[:4], refs[4:8], refs[8]
    copies = [pltpu.make_async_copy(a, b, sem.at[i]) for i, (a, b) in enumerate(zip(inputs, outs))]
    for copy in copies:
        copy.start()
    for copy in copies:
        copy.wait()


def solution(mesh):
    n_row, n_col = mesh.shape["row"], mesh.shape["col"]
    n_a, n_b = ROWS * n_col, n_row // ROWS
    vmem = pl.BlockSpec(memory_space=pltpu.VMEM)
    smem = pl.BlockSpec(memory_space=pltpu.SMEM)
    hbm = pl.BlockSpec(memory_space=pltpu.HBM)
    f32 = jnp.float32

    def pin(x):
        return pltpu.with_memory_space_constraint(x, pltpu.HBM)

    def per_device(pos, vel, acc, jerk, mass, time, steps, index, count):
        stars = pos.shape[1]
        strength = GRAVITY / (stars * n_row * n_col)
        arrays = (pos, vel, acc, jerk, mass, time, index)
        tgt, src, cnt = pl.pallas_call(
            functools.partial(exchange_kernel, n_row, n_col, strength),
            out_shape=(
                jax.ShapeDtypeStruct((n_a, 8, LANES), f32),
                jax.ShapeDtypeStruct((n_b, 8, stars), f32),
                jax.ShapeDtypeStruct((1, LANES), jnp.int32),
            ),
            in_specs=[smem, smem] + [hbm] * 7,
            out_specs=(vmem, vmem, vmem),
            scratch_shapes=[
                *[pltpu.VMEM(x.shape, x.dtype) for x in arrays],
                pltpu.SemaphoreType.DMA((7,)),
                pltpu.SemaphoreType.DMA((n_a,)),
                pltpu.SemaphoreType.DMA((n_a,)),
                pltpu.SemaphoreType.DMA((n_b,)),
                pltpu.SemaphoreType.DMA((n_b,)),
            ],
            compiler_params=pltpu.CompilerParams(
                collective_id=0, has_side_effects=True, vmem_limit_bytes=GRANT
            ),
            name="exchange",
        )(steps, count, *[pin(x) for x in arrays])
        chunks = n_b * stars // LANES
        part = pl.pallas_call(
            force_kernel,
            out_shape=jax.ShapeDtypeStruct((n_a, 8, LANES), f32),
            in_specs=[smem, vmem, vmem],
            out_specs=vmem,
            scratch_shapes=[
                pltpu.VMEM((n_a + 2, 8, LANES), f32),
                pltpu.VMEM((chunks * LANES, 96), jnp.bfloat16),
                pltpu.VMEM((chunks, 32, 2 * LANES), jnp.bfloat16),
            ],
            compiler_params=pltpu.CompilerParams(vmem_limit_bytes=2 * GRANT),
            name="forces",
        )(cnt, tgt, src)
        arrays = (pos, vel, acc, jerk, time, index)
        news = pl.pallas_call(
            functools.partial(return_kernel, n_row, n_col),
            out_shape=(jax.ShapeDtypeStruct(pos.shape, f32),) * 4,
            in_specs=[smem, smem, vmem] + [hbm] * 6,
            out_specs=(vmem,) * 4,
            scratch_shapes=[
                *[pltpu.VMEM(x.shape, x.dtype) for x in arrays],
                pltpu.SemaphoreType.DMA((6,)),
                pltpu.VMEM((n_a, 8, LANES), f32),
                pltpu.SemaphoreType.DMA((n_a,)),
                pltpu.SemaphoreType.DMA((n_a,)),
            ],
            compiler_params=pltpu.CompilerParams(
                collective_id=1, has_side_effects=True, vmem_limit_bytes=GRANT
            ),
            name="returns",
        )(steps, count, part, *[pin(x) for x in arrays])
        return pl.pallas_call(
            store_kernel,
            out_shape=(jax.ShapeDtypeStruct(pos.shape, f32),) * 4,
            in_specs=[vmem] * 4,
            out_specs=(hbm,) * 4,
            scratch_shapes=[pltpu.SemaphoreType.DMA((4,))],
            compiler_params=pltpu.CompilerParams(vmem_limit_bytes=GRANT),
            name="store",
        )(*news)

    both = ("row", "col")
    state = P(None, both)
    return jax.shard_map(
        per_device,
        mesh=mesh,
        in_specs=(state, state, state, state, P(both), P(both), P(), state, state),
        out_specs=(state, state, state, state),
        check_vma=False,
    )
```

```python
import functools
import math

import jax
import jax.numpy as jnp
from jax import lax
from jax.experimental import pallas as pl
from jax.experimental.pallas import tpu as pltpu
from jax.sharding import PartitionSpec as P

SOFTENING = 0.0025
GRAVITY = 8.0
LANES = 128
ROWS = 2
AHEAD = 2
SPAN = 3
GRANT = 8 << 20
MESH = pl.DeviceIdType.MESH
HIGHEST = lax.Precision.HIGHEST


def predict(pos, vel, acc, jerk, elapsed):
    square = elapsed * elapsed
    pred_pos = pos + vel * elapsed + acc * (square * 0.5) + jerk * (square * elapsed / 6.0)
    pred_vel = vel + acc * elapsed + jerk * (square * 0.5)
    return pred_pos, pred_vel


def near(step, size):
    return min(step, size - step)


def plane_peers(n_col):
    side = math.isqrt(n_col)
    row, col = lax.axis_index("row"), lax.axis_index("col")
    x, y, core = lax.div(col, side), lax.rem(col, side), lax.rem(row, ROWS)
    xs = [lax.rem(x + i, side) * side for i in range(side)]
    ys = [lax.rem(y + i, side) for i in range(side)]
    rows = [row - core + lax.rem(core + i, ROWS) for i in range(ROWS)]
    peers = []
    for i in range(ROWS):
        for j in range(side):
            for k in range(side):
                slot = (i * side + j) * side + k
                back = ((-i % ROWS) * side + (-j % side)) * side + (-k % side)
                far = near(j, side) + near(k, side)
                peers.append((far, slot, back, (rows[i], xs[j] + ys[k])))
    return sorted(peers[1:], key=lambda peer: -peer[0])


def line_peers(n_row):
    size = n_row // ROWS
    row, col = lax.axis_index("row"), lax.axis_index("col")
    place, core = lax.div(row, ROWS), lax.rem(row, ROWS)
    peers = [
        (near(i, size), i, size - i, (lax.rem(place + i, size) * ROWS + core, col))
        for i in range(1, size)
    ]
    return sorted(peers, key=lambda peer: -peer[0])


def greet(peers):
    barrier = pltpu.get_barrier_semaphore()
    for _, _, _, device in sorted(peers, key=lambda peer: -peer[0]):
        pl.semaphore_signal(barrier, inc=1, device_id=device, device_id_type=MESH)


def one_hot(index_row, count, stars):
    star = lax.broadcasted_iota(jnp.int32, (stars, LANES), 0)
    slot = lax.broadcasted_iota(jnp.int32, (stars, LANES), 1)
    return jnp.where((star == index_row) & (slot < count), 1.0, 0.0)


def exchange_kernel(
    n_row, n_col, strength,
    step_ref, count_ref, *refs,
):
    inputs, (tgt_ref, src_ref, cnt_ref), rest = refs[:7], refs[7:10], refs[10:]
    local, (load_sem, send_a, recv_a, send_b, recv_b) = rest[:7], rest[7:]
    pos_ref, vel_ref, acc_ref, jerk_ref, mass_ref, time_ref, index_ref = local
    n_a, n_b = ROWS * n_col, n_row // ROWS
    plane, line = plane_peers(n_col), line_peers(n_row)
    loads = [
        pltpu.make_async_copy(a, b, load_sem.at[i]) for i, (a, b) in enumerate(zip(inputs, local))
    ]
    for load in loads:
        load.start()
    greet(plane + line)
    for load in loads:
        load.wait()

    stars = pos_ref.shape[1]
    elapsed = step_ref[0] - time_ref[...].reshape(1, stars)
    pred_pos, pred_vel = predict(pos_ref[...], vel_ref[...], acc_ref[...], jerk_ref[...], elapsed)
    weight = mass_ref[...].reshape(1, stars) * strength
    packet = jnp.concatenate([pred_pos, pred_vel, weight, jnp.zeros_like(weight)], axis=0)
    src_ref[0] = packet
    count = count_ref[0, 0]
    chosen = jnp.dot(
        packet, one_hot(index_ref[...], LANES, stars), precision=HIGHEST,
        preferred_element_type=jnp.float32,
    )
    comp = lax.broadcasted_iota(jnp.int32, (8, LANES), 0)
    tgt_ref[0] = jnp.where(comp == 6, count.astype(jnp.float32), chosen)

    pl.semaphore_wait(pltpu.get_barrier_semaphore(), n_a + n_b - 2)
    far = [
        pltpu.make_async_remote_copy(
            src_ref=src_ref.at[0, 0:7], dst_ref=src_ref.at[back, 0:7],
            send_sem=send_b.at[slot], recv_sem=recv_b.at[back],
            device_id=device, device_id_type=MESH,
        )
        for _, slot, back, device in line
    ]
    wide = [
        pltpu.make_async_remote_copy(
            src_ref=tgt_ref.at[0, 0:7], dst_ref=tgt_ref.at[back, 0:7],
            send_sem=send_a.at[slot], recv_sem=recv_a.at[back],
            device_id=device, device_id_type=MESH,
        )
        for _, slot, back, device in plane
    ]
    for copy in far + wide:
        copy.start()
    for copy in wide:
        copy.wait()
    lane = lax.broadcasted_iota(jnp.int32, (1, LANES), 1)
    counts = jnp.zeros((1, LANES), jnp.float32)
    for k in range(n_a):
        counts = jnp.where(lane == k, tgt_ref[k, 6:7, :], counts)
    cnt_ref[...] = counts.astype(jnp.int32)
    for copy in far:
        copy.wait()


def split3(x):
    high = x.astype(jnp.bfloat16).astype(jnp.float32)
    rest = x - high
    mid = rest.astype(jnp.bfloat16).astype(jnp.float32)
    return high, mid, (rest - mid).astype(jnp.bfloat16).astype(jnp.float32)


def grid3(x):
    coarse = jnp.floor(x * 8.0 + 0.5) * 0.125
    rest = x - coarse
    fine = jnp.floor(rest * 4096.0 + 0.5) * (1.0 / 4096.0)
    return coarse, fine, (rest - fine).astype(jnp.bfloat16).astype(jnp.float32)


def sum3(x):
    return x[0:1] + x[1:2] + x[2:3]


def levels(state):
    xg, xm, xr = grid3(state[0:3])
    vh, vm, vl = split3(state[3:6])
    x, v = xg + xm + xr, vh + vm + vl
    scalars = [
        sum3(x * v),
        sum3(xg * xg + 2.0 * (xg * xm)),
        sum3(xm * xm + 2.0 * (xg * xr) + 2.0 * (xm * xr) + xr * xr),
    ]
    return (xg, xm, xr), (vh, vm, vl), scalars


def source_features(state):
    xs, vs, (s, ab, c) = levels(state)
    one = jnp.ones_like(state[0:1])
    none = jnp.zeros_like(one)
    s, ab, c = split3(s), split3(ab), split3(c)
    g = jnp.concatenate([xs[0], vs[0], s[0], one], axis=0)
    m = jnp.concatenate([xs[1], vs[1], s[1], none], axis=0)
    r = jnp.concatenate([xs[2], vs[2], s[2], none], axis=0)
    e = jnp.concatenate([*ab, one, none, none, none, none], axis=0)
    f = jnp.concatenate([*c, one, one, none, none, none], axis=0)
    return jnp.concatenate([g, g, m, e, g, m, m, r, r, r, f, jnp.zeros_like(f)], axis=0)


def target_features(state):
    xs, vs, (s, ab, c) = levels(state)
    one = jnp.ones_like(state[0:1])
    none = jnp.zeros_like(one)
    void = jnp.zeros_like(state[0:3])
    zero = jnp.zeros_like(state)
    s, ab, c = split3(s), split3(ab), split3(c + SOFTENING)
    x2 = [-2.0 * z for z in xs]
    xs, vs = [-z for z in xs], [-z for z in vs]

    def block(*rows):
        return jnp.concatenate(rows, axis=0)

    radial = block(
        vs[0], xs[0], one, s[0],
        vs[1], xs[1], none, s[1],
        vs[0], xs[0], one, none,
        zero,
        vs[2], xs[2], none, s[2],
        vs[1], xs[1], none, none,
        zero,
        vs[0], xs[0], one, none,
        zero, zero, zero, zero,
    )
    square = block(
        x2[0], void, none, ab[0],
        x2[1], void, none, ab[1],
        x2[0], void, none, none,
        one, one, one, ab[2], void, none,
        x2[2], void, none, c[0],
        x2[1], void, none, none,
        x2[2], void, none, none,
        x2[0], void, none, none,
        x2[1], void, none, none,
        x2[2], void, none, none,
        one, one, one, c[1], c[2], void,
        zero,
    )
    return jnp.concatenate([radial, square], axis=1).astype(jnp.bfloat16)


def force_kernel(cnt_in, tgt_ref, src_ref, out_ref, dense, src_t, packed, cnt_ref, cnt_sem):
    load = pltpu.make_async_copy(cnt_in, cnt_ref, cnt_sem)
    load.start()
    n_a, n_b, stars = tgt_ref.shape[0], src_ref.shape[0], src_ref.shape[2]
    per = stars // LANES
    parts = n_b * per
    f32, bf16 = jnp.float32, jnp.bfloat16
    comp = lax.broadcasted_iota(jnp.int32, (8, LANES), 0)
    lane = lax.broadcasted_iota(jnp.int32, (8, LANES), 1)

    def piece(j):
        b, p = j // per, j % per
        return src_ref[b, :, p * LANES : (p + 1) * LANES]

    top = bottom = piece(0)
    for j in range(1, parts):
        top, bottom = jnp.maximum(top, piece(j)), jnp.minimum(bottom, piece(j))
    middle = jnp.max(top, axis=1, keepdims=True) + jnp.min(bottom, axis=1, keepdims=True)
    middle = jnp.where(comp < 6, jnp.broadcast_to(0.5 * middle, (8, LANES)), 0.0)

    for j in range(parts):
        if j == parts // 2:
            load.wait()
        state = piece(j) - middle
        src_t[j * LANES : (j + 1) * LANES, :] = source_features(state).T.astype(bf16)
        moment = jnp.where(comp < 6, state * state[6:7], jnp.where(comp == 6, state, 0.0))
        high, mid, low = split3(moment)
        rows = jnp.concatenate([high, mid, low, jnp.zeros((8, LANES), f32)], axis=0).astype(bf16)
        packed[j, :, 0:LANES] = rows
        packed[j, :, LANES : 2 * LANES] = rows

    count = jnp.int32(0)
    front = tgt_ref[0]
    starts = []
    for k in range(n_a):
        starts.append(count)
        tile, shift = lax.div(count, LANES), lax.rem(count, LANES)
        rolled = pltpu.roll(tgt_ref[k], shift, 1)
        merged = jnp.where(lane >= shift, rolled, front)
        dense[tile] = merged
        dense[tile + 1] = rolled
        count = count + cnt_ref[0, k]
        front = jnp.where(lax.div(count, LANES) == tile, merged, rolled)
    tiles = (count + LANES - 1) // LANES

    def tile_step(t, _):
        state = dense[t] - middle
        pair = target_features(state)

        def products_of(c):
            left = src_t[c * SPAN * LANES : (c + 1) * SPAN * LANES, :]
            return [
                jnp.dot(left, pair[:, :LANES], preferred_element_type=f32),
                jnp.dot(left, pair[:, LANES:], preferred_element_type=f32),
            ]

        def weights_of(prod, at):
            tiles_of = [[], [], [], []]
            for g in range(8):
                pulls, twists = [], []
                for h in range(2):
                    row = slice(at + 16 * g + 8 * h, at + 16 * g + 8 * h + 8)
                    radial = prod[0][row]
                    inv = lax.rsqrt(prod[1][row])
                    inv2 = inv * inv
                    pull = inv * inv2
                    pulls.append(pull)
                    twists.append((radial * inv2) * pull)
                for s, both in enumerate((pulls, twists)):
                    full = jnp.concatenate(both, axis=0)
                    high = full.astype(bf16)
                    tiles_of[s].append(high)
                    tiles_of[2 + s].append((full - high.astype(f32)).astype(bf16))
            return [jnp.concatenate(tiles_of[s] + tiles_of[2 + s], axis=0) for s in range(2)]

        acc = [jnp.zeros((32, LANES), f32)] * 2
        groups = parts // SPAN
        ahead = [products_of(c) for c in range(AHEAD)]
        right = None
        for c in range(groups):
            if c + AHEAD < groups:
                ahead.append(products_of(c + AHEAD))
            for u in range(SPAN):
                last, right = right, weights_of(ahead[c], u * LANES)
                if last is not None:
                    acc = [
                        z + jnp.dot(packed[c * SPAN + u - 1], w, preferred_element_type=f32)
                        for z, w in zip(acc, last)
                    ]
        acc = [
            z + jnp.dot(packed[parts - 1], w, preferred_element_type=f32)
            for z, w in zip(acc, right)
        ]
        pull, twist = [z[0:8] + (z[8:16] + z[16:24]) for z in acc]
        force = pull - state * pull[6:7]
        tide = twist - state * twist[6:7]
        jerk = force[3:6] - 3.0 * tide[0:3]
        dense[t] = jnp.concatenate([force[0:3], jerk, jnp.zeros((2, LANES), f32)], axis=0)
        return 0

    lax.fori_loop(0, tiles, tile_step, 0)

    for k in range(n_a):
        tile, shift = lax.div(starts[k], LANES), lax.rem(starts[k], LANES)
        both = jnp.where(lane >= shift, dense[tile], dense[tile + 1])
        out_ref[k] = pltpu.roll(both, lax.rem(LANES - shift, LANES), 1)


def return_kernel(n_row, n_col, step_ref, count_ref, part_ref, *refs):
    inputs, outs, rest = refs[:6], refs[6:10], refs[10:]
    local, (load_sem, inbox, send_sem, recv_sem) = rest[:6], rest[6:]
    pos_ref, vel_ref, acc_ref, jerk_ref, time_ref, index_ref = local
    n_a = ROWS * n_col
    loads = [
        pltpu.make_async_copy(a, b, load_sem.at[i]) for i, (a, b) in enumerate(zip(inputs, local))
    ]
    peers = plane_peers(n_col)
    greet(peers)
    for load in loads:
        load.start()
    for load in loads:
        load.wait()
    stars = pos_ref.shape[1]
    pos, vel, acc, jerk = pos_ref[...], vel_ref[...], acc_ref[...], jerk_ref[...]
    span = step_ref[0] - time_ref[...].reshape(1, stars)
    pred_pos, pred_vel = predict(pos, vel, acc, jerk, span)
    pick = one_hot(index_ref[...], count_ref[0, 0], stars)
    pl.semaphore_wait(pltpu.get_barrier_semaphore(), n_a - 1)
    copies = [
        pltpu.make_async_remote_copy(
            src_ref=part_ref.at[slot, 0:6], dst_ref=inbox.at[back, 0:6],
            send_sem=send_sem.at[slot], recv_sem=recv_sem.at[back],
            device_id=device, device_id_type=MESH,
        )
        for _, slot, back, device in peers
    ]
    for copy in copies:
        copy.start()
    for copy in copies:
        copy.wait()
    total = part_ref[0]
    for k in range(1, n_a):
        total = total + inbox[k]
    comp = lax.broadcasted_iota(jnp.int32, (8, LANES), 0)
    total = jnp.where(comp < 6, total, 1.0)
    placed = lax.dot_general(
        total, pick, (((1,), (1,)), ((), ())), precision=HIGHEST,
        preferred_element_type=jnp.float32,
    )
    active = placed[6:7] > 0.5
    acc1, jerk1 = placed[0:3], placed[3:6]
    change = acc - acc1
    snap = -6.0 * change - span * (4.0 * jerk + 2.0 * jerk1)
    crack = 12.0 * change + 6.0 * span * (jerk + jerk1)
    out_pos = pred_pos + span * span * (snap / 24.0 + crack / 120.0)
    out_vel = pred_vel + span * (snap / 6.0 + crack / 24.0)
    outs[0][...] = jnp.where(active, out_pos, pos)
    outs[1][...] = jnp.where(active, out_vel, vel)
    outs[2][...] = jnp.where(active, acc1, acc)
    outs[3][...] = jnp.where(active, jerk1, jerk)


def store_kernel(*refs):
    inputs, outs, sem = refs[:4], refs[4:8], refs[8]
    copies = [pltpu.make_async_copy(a, b, sem.at[i]) for i, (a, b) in enumerate(zip(inputs, outs))]
    for copy in copies:
        copy.start()
    for copy in copies:
        copy.wait()


def solution(mesh):
    n_row, n_col = mesh.shape["row"], mesh.shape["col"]
    n_a, n_b = ROWS * n_col, n_row // ROWS
    vmem = pl.BlockSpec(memory_space=pltpu.VMEM)
    smem = pl.BlockSpec(memory_space=pltpu.SMEM)
    hbm = pl.BlockSpec(memory_space=pltpu.HBM)
    f32 = jnp.float32

    def pin(x):
        return pltpu.with_memory_space_constraint(x, pltpu.HBM)

    def per_device(pos, vel, acc, jerk, mass, time, steps, index, count):
        stars = pos.shape[1]
        strength = GRAVITY / (stars * n_row * n_col)
        arrays = (pos, vel, acc, jerk, mass, time, index)
        tgt, src, cnt = pl.pallas_call(
            functools.partial(exchange_kernel, n_row, n_col, strength),
            out_shape=(
                jax.ShapeDtypeStruct((n_a, 8, LANES), f32),
                jax.ShapeDtypeStruct((n_b, 8, stars), f32),
                jax.ShapeDtypeStruct((1, LANES), jnp.int32),
            ),
            in_specs=[smem, smem] + [hbm] * 7,
            out_specs=(vmem, vmem, vmem),
            scratch_shapes=[
                *[pltpu.VMEM(x.shape, x.dtype) for x in arrays],
                pltpu.SemaphoreType.DMA((7,)),
                pltpu.SemaphoreType.DMA((n_a,)),
                pltpu.SemaphoreType.DMA((n_a,)),
                pltpu.SemaphoreType.DMA((n_b,)),
                pltpu.SemaphoreType.DMA((n_b,)),
            ],
            compiler_params=pltpu.CompilerParams(
                collective_id=0, has_side_effects=True, vmem_limit_bytes=GRANT
            ),
            name="exchange",
        )(steps, count, *[pin(x) for x in arrays])
        chunks = n_b * stars // LANES
        part = pl.pallas_call(
            force_kernel,
            out_shape=jax.ShapeDtypeStruct((n_a, 8, LANES), f32),
            in_specs=[pl.BlockSpec(memory_space=pl.ANY), vmem, vmem],
            out_specs=vmem,
            scratch_shapes=[
                pltpu.VMEM((n_a + 2, 8, LANES), f32),
                pltpu.VMEM((chunks * LANES, 96), jnp.bfloat16),
                pltpu.VMEM((chunks, 32, 2 * LANES), jnp.bfloat16),
                pltpu.SMEM((1, LANES), jnp.int32),
                pltpu.SemaphoreType.DMA,
            ],
            compiler_params=pltpu.CompilerParams(vmem_limit_bytes=2 * GRANT),
            name="forces",
        )(cnt, tgt, src)
        arrays = (pos, vel, acc, jerk, time, index)
        news = pl.pallas_call(
            functools.partial(return_kernel, n_row, n_col),
            out_shape=(jax.ShapeDtypeStruct(pos.shape, f32),) * 4,
            in_specs=[smem, smem, vmem] + [hbm] * 6,
            out_specs=(vmem,) * 4,
            scratch_shapes=[
                *[pltpu.VMEM(x.shape, x.dtype) for x in arrays],
                pltpu.SemaphoreType.DMA((6,)),
                pltpu.VMEM((n_a, 8, LANES), f32),
                pltpu.SemaphoreType.DMA((n_a,)),
                pltpu.SemaphoreType.DMA((n_a,)),
            ],
            compiler_params=pltpu.CompilerParams(
                collective_id=1, has_side_effects=True, vmem_limit_bytes=GRANT
            ),
            name="returns",
        )(steps, count, part, *[pin(x) for x in arrays])
        return pl.pallas_call(
            store_kernel,
            out_shape=(jax.ShapeDtypeStruct(pos.shape, f32),) * 4,
            in_specs=[vmem] * 4,
            out_specs=(hbm,) * 4,
            scratch_shapes=[pltpu.SemaphoreType.DMA((4,))],
            compiler_params=pltpu.CompilerParams(vmem_limit_bytes=GRANT),
            name="store",
        )(*news)

    both = ("row", "col")
    state = P(None, both)
    return jax.shard_map(
        per_device,
        mesh=mesh,
        in_specs=(state, state, state, state, P(both), P(both), P(), state, state),
        out_specs=(state, state, state, state),
        check_vma=False,
    )
```

```python
import functools
import math

import jax
import jax.numpy as jnp
from jax import lax
from jax.experimental import pallas as pl
from jax.experimental.pallas import tpu as pltpu
from jax.sharding import PartitionSpec as P

SOFTENING = 0.0025
GRAVITY = 8.0
LANES = 128
ROWS = 2
AHEAD = 2
SPAN = 3
GRANT = 8 << 20
MESH = pl.DeviceIdType.MESH
HIGHEST = lax.Precision.HIGHEST


def predict(pos, vel, acc, jerk, elapsed):
    square = elapsed * elapsed
    pred_pos = pos + vel * elapsed + acc * (square * 0.5) + jerk * (square * elapsed / 6.0)
    pred_vel = vel + acc * elapsed + jerk * (square * 0.5)
    return pred_pos, pred_vel


def near(step, size):
    return min(step, size - step)


def plane_peers(n_col):
    side = math.isqrt(n_col)
    row, col = lax.axis_index("row"), lax.axis_index("col")
    x, y, core = lax.div(col, side), lax.rem(col, side), lax.rem(row, ROWS)
    xs = [lax.rem(x + i, side) * side for i in range(side)]
    ys = [lax.rem(y + i, side) for i in range(side)]
    rows = [row - core + lax.rem(core + i, ROWS) for i in range(ROWS)]
    peers = []
    for i in range(ROWS):
        for j in range(side):
            for k in range(side):
                slot = (i * side + j) * side + k
                back = ((-i % ROWS) * side + (-j % side)) * side + (-k % side)
                far = near(j, side) + near(k, side)
                peers.append((far, slot, back, (rows[i], xs[j] + ys[k])))
    return sorted(peers[1:], key=lambda peer: -peer[0])


def line_peers(n_row):
    size = n_row // ROWS
    row, col = lax.axis_index("row"), lax.axis_index("col")
    place, core = lax.div(row, ROWS), lax.rem(row, ROWS)
    peers = [
        (near(i, size), i, size - i, (lax.rem(place + i, size) * ROWS + core, col))
        for i in range(1, size)
    ]
    return sorted(peers, key=lambda peer: -peer[0])


def greet(peers):
    barrier = pltpu.get_barrier_semaphore()
    for _, _, _, device in sorted(peers, key=lambda peer: -peer[0]):
        pl.semaphore_signal(barrier, inc=1, device_id=device, device_id_type=MESH)


def one_hot(index_row, count, stars):
    star = lax.broadcasted_iota(jnp.int32, (stars, LANES), 0)
    slot = lax.broadcasted_iota(jnp.int32, (stars, LANES), 1)
    return jnp.where((star == index_row) & (slot < count), 1.0, 0.0)


def exchange_kernel(
    n_row, n_col, strength,
    step_ref, count_ref, *refs,
):
    inputs, (tgt_ref, src_ref, cnt_ref), rest = refs[:7], refs[7:10], refs[10:]
    local, (load_sem, send_a, recv_a, send_b, recv_b) = rest[:7], rest[7:]
    pos_ref, vel_ref, acc_ref, jerk_ref, mass_ref, time_ref, index_ref = local
    n_a, n_b = ROWS * n_col, n_row // ROWS
    plane, line = plane_peers(n_col), line_peers(n_row)
    loads = [
        pltpu.make_async_copy(a, b, load_sem.at[i]) for i, (a, b) in enumerate(zip(inputs, local))
    ]
    for load in loads:
        load.start()
    greet(plane + line)
    for load in loads:
        load.wait()

    stars = pos_ref.shape[1]
    elapsed = step_ref[0] - time_ref[...].reshape(1, stars)
    pred_pos, pred_vel = predict(pos_ref[...], vel_ref[...], acc_ref[...], jerk_ref[...], elapsed)
    weight = mass_ref[...].reshape(1, stars) * strength
    packet = jnp.concatenate([pred_pos, pred_vel, weight, jnp.zeros_like(weight)], axis=0)
    src_ref[0] = packet
    count = count_ref[0, 0]
    chosen = jnp.dot(
        packet, one_hot(index_ref[...], LANES, stars), precision=HIGHEST,
        preferred_element_type=jnp.float32,
    )
    comp = lax.broadcasted_iota(jnp.int32, (8, LANES), 0)
    tgt_ref[0] = jnp.where(comp == 6, count.astype(jnp.float32), chosen)

    pl.semaphore_wait(pltpu.get_barrier_semaphore(), n_a + n_b - 2)
    far = [
        pltpu.make_async_remote_copy(
            src_ref=src_ref.at[0, 0:7], dst_ref=src_ref.at[back, 0:7],
            send_sem=send_b.at[slot], recv_sem=recv_b.at[back],
            device_id=device, device_id_type=MESH,
        )
        for _, slot, back, device in line
    ]
    wide = [
        pltpu.make_async_remote_copy(
            src_ref=tgt_ref.at[0, 0:7], dst_ref=tgt_ref.at[back, 0:7],
            send_sem=send_a.at[slot], recv_sem=recv_a.at[back],
            device_id=device, device_id_type=MESH,
        )
        for _, slot, back, device in plane
    ]
    for copy in far + wide:
        copy.start()
    for copy in wide:
        copy.wait()
    lane = lax.broadcasted_iota(jnp.int32, (1, LANES), 1)
    counts = jnp.zeros((1, LANES), jnp.float32)
    for k in range(n_a):
        counts = jnp.where(lane == k, tgt_ref[k, 6:7, :], counts)
    cnt_ref[...] = counts.astype(jnp.int32)
    for copy in far:
        copy.wait()


def split3(x):
    high = x.astype(jnp.bfloat16).astype(jnp.float32)
    rest = x - high
    mid = rest.astype(jnp.bfloat16).astype(jnp.float32)
    return high, mid, (rest - mid).astype(jnp.bfloat16).astype(jnp.float32)


def grid3(x):
    coarse = jnp.floor(x * 8.0 + 0.5) * 0.125
    rest = x - coarse
    fine = jnp.floor(rest * 4096.0 + 0.5) * (1.0 / 4096.0)
    return coarse, fine, (rest - fine).astype(jnp.bfloat16).astype(jnp.float32)


def sum3(x):
    return x[0:1] + x[1:2] + x[2:3]


def levels(state):
    xg, xm, xr = grid3(state[0:3])
    vh, vm, vl = split3(state[3:6])
    x, v = xg + xm + xr, vh + vm + vl
    scalars = [
        sum3(x * v),
        sum3(xg * xg + 2.0 * (xg * xm)),
        sum3(xm * xm + 2.0 * (xg * xr) + 2.0 * (xm * xr) + xr * xr),
    ]
    return (xg, xm, xr), (vh, vm, vl), scalars


def source_features(state):
    xs, vs, (s, ab, c) = levels(state)
    one = jnp.ones_like(state[0:1])
    none = jnp.zeros_like(one)
    s, ab, c = split3(s), split3(ab), split3(c)
    g = jnp.concatenate([xs[0], vs[0], s[0], one], axis=0)
    m = jnp.concatenate([xs[1], vs[1], s[1], none], axis=0)
    r = jnp.concatenate([xs[2], vs[2], s[2], none], axis=0)
    e = jnp.concatenate([*ab, one, none, none, none, none], axis=0)
    f = jnp.concatenate([*c, one, one, none, none, none], axis=0)
    return jnp.concatenate([g, g, m, e, g, m, m, r, r, r, f, jnp.zeros_like(f)], axis=0)


def target_features(state):
    xs, vs, (s, ab, c) = levels(state)
    one = jnp.ones_like(state[0:1])
    none = jnp.zeros_like(one)
    void = jnp.zeros_like(state[0:3])
    zero = jnp.zeros_like(state)
    s, ab, c = split3(s), split3(ab), split3(c + SOFTENING)
    x2 = [-2.0 * z for z in xs]
    xs, vs = [-z for z in xs], [-z for z in vs]

    def block(*rows):
        return jnp.concatenate(rows, axis=0)

    radial = block(
        vs[0], xs[0], one, s[0],
        vs[1], xs[1], none, s[1],
        vs[0], xs[0], one, none,
        zero,
        vs[2], xs[2], none, s[2],
        vs[1], xs[1], none, none,
        zero,
        vs[0], xs[0], one, none,
        zero, zero, zero, zero,
    )
    square = block(
        x2[0], void, none, ab[0],
        x2[1], void, none, ab[1],
        x2[0], void, none, none,
        one, one, one, ab[2], void, none,
        x2[2], void, none, c[0],
        x2[1], void, none, none,
        x2[2], void, none, none,
        x2[0], void, none, none,
        x2[1], void, none, none,
        x2[2], void, none, none,
        one, one, one, c[1], c[2], void,
        zero,
    )
    return jnp.concatenate([radial, square], axis=1).astype(jnp.bfloat16)


def force_kernel(cnt_in, tgt_ref, src_ref, out_ref, dense, src_t, packed, cnt_ref, cnt_sem):
    load = pltpu.make_async_copy(cnt_in, cnt_ref, cnt_sem)
    load.start()
    n_a, n_b, stars = tgt_ref.shape[0], src_ref.shape[0], src_ref.shape[2]
    per = stars // LANES
    parts = n_b * per
    f32, bf16 = jnp.float32, jnp.bfloat16
    comp = lax.broadcasted_iota(jnp.int32, (8, LANES), 0)
    lane = lax.broadcasted_iota(jnp.int32, (8, LANES), 1)

    def piece(j):
        b, p = j // per, j % per
        return src_ref[b, :, p * LANES : (p + 1) * LANES]

    top = bottom = piece(0)
    for j in range(1, parts):
        top, bottom = jnp.maximum(top, piece(j)), jnp.minimum(bottom, piece(j))
    middle = jnp.max(top, axis=1, keepdims=True) + jnp.min(bottom, axis=1, keepdims=True)
    middle = jnp.where(comp < 6, jnp.broadcast_to(0.5 * middle, (8, LANES)), 0.0)

    for j in range(parts):
        if j == parts // 2:
            load.wait()
        state = piece(j) - middle
        src_t[j * LANES : (j + 1) * LANES, :] = source_features(state).T.astype(bf16)
        moment = jnp.where(comp < 6, state * state[6:7], jnp.where(comp == 6, state, 0.0))
        high, mid, low = split3(moment)
        rows = jnp.concatenate([high, mid, low, jnp.zeros((8, LANES), f32)], axis=0).astype(bf16)
        packed[j, :, 0:LANES] = rows
        packed[j, :, LANES : 2 * LANES] = rows

    count = jnp.int32(0)
    front = tgt_ref[0]
    starts = []
    for k in range(n_a):
        starts.append(count)
        tile, shift = lax.div(count, LANES), lax.rem(count, LANES)
        rolled = pltpu.roll(tgt_ref[k], shift, 1)
        merged = jnp.where(lane >= shift, rolled, front)
        dense[tile] = merged
        dense[tile + 1] = rolled
        count = count + cnt_ref[0, k]
        front = jnp.where(lax.div(count, LANES) == tile, merged, rolled)
    tiles = (count + LANES - 1) // LANES

    def tile_step(t, _):
        state = dense[t] - middle
        pair = target_features(state)

        def products_of(c):
            left = src_t[c * SPAN * LANES : (c + 1) * SPAN * LANES, :]
            return [
                jnp.dot(left, pair[:, :LANES], preferred_element_type=f32),
                jnp.dot(left, pair[:, LANES:], preferred_element_type=f32),
            ]

        def weights_of(prod, at):
            tiles_of = [[], [], [], []]
            for g in range(8):
                pulls, twists = [], []
                for h in range(2):
                    row = slice(at + 16 * g + 8 * h, at + 16 * g + 8 * h + 8)
                    radial = prod[0][row]
                    inv = lax.rsqrt(prod[1][row])
                    inv2 = inv * inv
                    pull = inv * inv2
                    pulls.append(pull)
                    twists.append((radial * inv2) * pull)
                for s, both in enumerate((pulls, twists)):
                    full = jnp.concatenate(both, axis=0)
                    high = full.astype(bf16)
                    tiles_of[s].append(high)
                    tiles_of[2 + s].append((full - high.astype(f32)).astype(bf16))
            return [jnp.concatenate(tiles_of[s] + tiles_of[2 + s], axis=0) for s in range(2)]

        acc = [jnp.zeros((32, LANES), f32)] * 2
        groups = parts // SPAN
        ahead = [products_of(c) for c in range(AHEAD)]
        right = None
        for c in range(groups):
            if c + AHEAD < groups:
                ahead.append(products_of(c + AHEAD))
            for u in range(SPAN):
                last, right = right, weights_of(ahead[c], u * LANES)
                if last is not None:
                    acc = [
                        z + jnp.dot(packed[c * SPAN + u - 1], w, preferred_element_type=f32)
                        for z, w in zip(acc, last)
                    ]
        acc = [
            z + jnp.dot(packed[parts - 1], w, preferred_element_type=f32)
            for z, w in zip(acc, right)
        ]
        pull, twist = [z[0:8] + (z[8:16] + z[16:24]) for z in acc]
        force = pull - state * pull[6:7]
        tide = twist - state * twist[6:7]
        jerk = force[3:6] - 3.0 * tide[0:3]
        dense[t] = jnp.concatenate([force[0:3], jerk, jnp.zeros((2, LANES), f32)], axis=0)
        return 0

    lax.fori_loop(0, tiles, tile_step, 0)

    for k in range(n_a):
        tile, shift = lax.div(starts[k], LANES), lax.rem(starts[k], LANES)
        both = jnp.where(lane >= shift, dense[tile], dense[tile + 1])
        out_ref[k] = pltpu.roll(both, lax.rem(LANES - shift, LANES), 1)


def return_kernel(n_row, n_col, step_ref, count_ref, part_ref, *refs):
    inputs, outs, rest = refs[:6], refs[6:10], refs[10:]
    local, (load_sem, inbox, send_sem, recv_sem) = rest[:6], rest[6:]
    pos_ref, vel_ref, acc_ref, jerk_ref, time_ref, index_ref = local
    n_a = ROWS * n_col
    loads = [
        pltpu.make_async_copy(a, b, load_sem.at[i]) for i, (a, b) in enumerate(zip(inputs, local))
    ]
    peers = plane_peers(n_col)
    greet(peers)
    for load in loads:
        load.start()
    for load in loads:
        load.wait()
    stars = pos_ref.shape[1]
    pos, vel, acc, jerk = pos_ref[...], vel_ref[...], acc_ref[...], jerk_ref[...]
    span = step_ref[0] - time_ref[...].reshape(1, stars)
    pred_pos, pred_vel = predict(pos, vel, acc, jerk, span)
    pick = one_hot(index_ref[...], count_ref[0, 0], stars).T.astype(jnp.bfloat16)
    pl.semaphore_wait(pltpu.get_barrier_semaphore(), n_a - 1)
    copies = [
        pltpu.make_async_remote_copy(
            src_ref=part_ref.at[slot, 0:6], dst_ref=inbox.at[back, 0:6],
            send_sem=send_sem.at[slot], recv_sem=recv_sem.at[back],
            device_id=device, device_id_type=MESH,
        )
        for _, slot, back, device in peers
    ]
    for copy in copies:
        copy.start()
    for copy in copies:
        copy.wait()
    terms = [part_ref[0]] + [inbox[k] for k in range(1, n_a)]
    while len(terms) > 1:
        terms = [sum(terms[i : i + 2]) for i in range(0, len(terms), 2)]
    comp = lax.broadcasted_iota(jnp.int32, (8, LANES), 0)
    halves = jnp.concatenate(split3(jnp.where(comp < 6, terms[0], 1.0)), axis=0)
    placed = jnp.dot(halves.astype(jnp.bfloat16), pick, preferred_element_type=jnp.float32)
    placed = (placed[0:8] + placed[8:16]) + placed[16:24]
    active = placed[6:7] > 0.5
    acc1, jerk1 = placed[0:3], placed[3:6]
    change = acc - acc1
    snap = -6.0 * change - span * (4.0 * jerk + 2.0 * jerk1)
    crack = 12.0 * change + 6.0 * span * (jerk + jerk1)
    out_pos = pred_pos + span * span * (snap / 24.0 + crack / 120.0)
    out_vel = pred_vel + span * (snap / 6.0 + crack / 24.0)
    outs[0][...] = jnp.where(active, out_pos, pos)
    outs[1][...] = jnp.where(active, out_vel, vel)
    outs[2][...] = jnp.where(active, acc1, acc)
    outs[3][...] = jnp.where(active, jerk1, jerk)


def store_kernel(*refs):
    inputs, outs, sem = refs[:4], refs[4:8], refs[8]
    copies = [pltpu.make_async_copy(a, b, sem.at[i]) for i, (a, b) in enumerate(zip(inputs, outs))]
    for copy in copies:
        copy.start()
    for copy in copies:
        copy.wait()


def solution(mesh):
    n_row, n_col = mesh.shape["row"], mesh.shape["col"]
    n_a, n_b = ROWS * n_col, n_row // ROWS
    vmem = pl.BlockSpec(memory_space=pltpu.VMEM)
    smem = pl.BlockSpec(memory_space=pltpu.SMEM)
    hbm = pl.BlockSpec(memory_space=pltpu.HBM)
    f32 = jnp.float32

    def pin(x):
        return pltpu.with_memory_space_constraint(x, pltpu.HBM)

    def per_device(pos, vel, acc, jerk, mass, time, steps, index, count):
        stars = pos.shape[1]
        strength = GRAVITY / (stars * n_row * n_col)
        arrays = (pos, vel, acc, jerk, mass, time, index)
        tgt, src, cnt = pl.pallas_call(
            functools.partial(exchange_kernel, n_row, n_col, strength),
            out_shape=(
                jax.ShapeDtypeStruct((n_a, 8, LANES), f32),
                jax.ShapeDtypeStruct((n_b, 8, stars), f32),
                jax.ShapeDtypeStruct((1, LANES), jnp.int32),
            ),
            in_specs=[smem, smem] + [hbm] * 7,
            out_specs=(vmem, vmem, vmem),
            scratch_shapes=[
                *[pltpu.VMEM(x.shape, x.dtype) for x in arrays],
                pltpu.SemaphoreType.DMA((7,)),
                pltpu.SemaphoreType.DMA((n_a,)),
                pltpu.SemaphoreType.DMA((n_a,)),
                pltpu.SemaphoreType.DMA((n_b,)),
                pltpu.SemaphoreType.DMA((n_b,)),
            ],
            compiler_params=pltpu.CompilerParams(
                collective_id=0, has_side_effects=True, vmem_limit_bytes=GRANT
            ),
            name="exchange",
        )(steps, count, *[pin(x) for x in arrays])
        chunks = n_b * stars // LANES
        part = pl.pallas_call(
            force_kernel,
            out_shape=jax.ShapeDtypeStruct((n_a, 8, LANES), f32),
            in_specs=[pl.BlockSpec(memory_space=pl.ANY), vmem, vmem],
            out_specs=vmem,
            scratch_shapes=[
                pltpu.VMEM((n_a + 2, 8, LANES), f32),
                pltpu.VMEM((chunks * LANES, 96), jnp.bfloat16),
                pltpu.VMEM((chunks, 32, 2 * LANES), jnp.bfloat16),
                pltpu.SMEM((1, LANES), jnp.int32),
                pltpu.SemaphoreType.DMA,
            ],
            compiler_params=pltpu.CompilerParams(vmem_limit_bytes=2 * GRANT),
            name="forces",
        )(cnt, tgt, src)
        arrays = (pos, vel, acc, jerk, time, index)
        news = pl.pallas_call(
            functools.partial(return_kernel, n_row, n_col),
            out_shape=(jax.ShapeDtypeStruct(pos.shape, f32),) * 4,
            in_specs=[smem, smem, vmem] + [hbm] * 6,
            out_specs=(vmem,) * 4,
            scratch_shapes=[
                *[pltpu.VMEM(x.shape, x.dtype) for x in arrays],
                pltpu.SemaphoreType.DMA((6,)),
                pltpu.VMEM((n_a, 8, LANES), f32),
                pltpu.SemaphoreType.DMA((n_a,)),
                pltpu.SemaphoreType.DMA((n_a,)),
            ],
            compiler_params=pltpu.CompilerParams(
                collective_id=1, has_side_effects=True, vmem_limit_bytes=GRANT
            ),
            name="returns",
        )(steps, count, part, *[pin(x) for x in arrays])
        return pl.pallas_call(
            store_kernel,
            out_shape=(jax.ShapeDtypeStruct(pos.shape, f32),) * 4,
            in_specs=[vmem] * 4,
            out_specs=(hbm,) * 4,
            scratch_shapes=[pltpu.SemaphoreType.DMA((4,))],
            compiler_params=pltpu.CompilerParams(vmem_limit_bytes=GRANT),
            name="store",
        )(*news)

    both = ("row", "col")
    state = P(None, both)
    return jax.shard_map(
        per_device,
        mesh=mesh,
        in_specs=(state, state, state, state, P(both), P(both), P(), state, state),
        out_specs=(state, state, state, state),
        check_vma=False,
    )
```
